1024 devices in a mesh: loop: 32 (over y_hi, x, core), section: 32 (over y_lo, z).
Axes of the slice: x: 8, y: 8 (y_hi: 2, y_lo: 4; y = y_hi * 4 + y_lo), z: 8, core: 2. Of those that a mesh axis runs over, the one named last changes fastest.
Arguments:
- features: bfloat16 [32, 64, 128, 512], P('loop', 'section'), may hold values from -6 to 6
- weight: bfloat16 [512, 512], replicated, may hold values from -0.25 to 0.25
- edge_tiles: bfloat16 [32, 64, 9, 128, 128], P('loop', 'section')
- block_list: int32 [32, 64, 9], P('loop', 'section'), may hold values from 0 to 8, as said below
- block_count: int32 [32, 64], P('loop', 'section'), may hold values from 1 to 9, as said below
- grad_hidden: bfloat16 [32, 64, 128, 512], P('loop', 'section'), may hold values from -6 to 6
Outputs:
- hidden: bfloat16 [32, 64, 128, 512], P('loop', 'section')
- grad_features: bfloat16 [32, 64, 128, 512], P('loop', 'section')
- grad_weight: float32 [512, 512], replicated
The draws below stay inside these ranges and needn't reach their ends.
Inputs may be any that keep to these rules, and one draw needn't show every extreme that they name: block_list[a, b] holds the block_count[a, b] slots whose tiles are nonzero, distinct and ascending, then the self slot 4 repeated; slot 4 is always listed; no slot points outside the grid. The pattern is symmetric: slot s of tile (a, b) is listed exactly when slot 8 - s of tile (a + u - 1, b + v - 1) is, and then edge_tiles of the one is the transpose of edge_tiles of the other; edge_tiles of slot 4 is symmetric. `block_count`: some tile row has all 9 tiles nonzero.
All inputs are finite; a program needn't handle non-finite values.
Results may differ from the reference program's by a relative error of at most 0.0059.
Values may be sent and summed in bfloat16 or wider, within the bound.
A program may use at most 32 MiB of HBM per device.

```python
import math
import jax
import jax.numpy as jnp

F = 512
TILE = 128
NTL = 32
NTS = 64
NODES = 262144


def pattern_draw(key):
    base_key = jax.random.fold_in(key, 11)
    rows = jnp.arange(NTL, dtype=jnp.int32)[:, None]
    cols = jnp.arange(NTS, dtype=jnp.int32)[None, :]
    offset = jax.random.randint(jax.random.fold_in(base_key, 1), (), 0, NTL)
    limit = 15 + 80 * ((rows + offset) % NTL) // NTL
    rolls = jax.random.randint(jax.random.fold_in(base_key, 2), (NTL, NTS, 9), 0, 100)
    upper = rolls < limit[:, :, None]
    columns = []
    for slot in range(9):
        row_off = slot // 3 - 1
        col_off = slot % 3 - 1
        inside = (rows + row_off >= 0) & (rows + row_off < NTL) & (cols + col_off >= 0) & (cols + col_off < NTS)
        if slot < 4:
            forced = (rows == 1) & (cols == 1) | (rows + row_off == 1) & (cols + col_off == 1)
            present = upper[:, :, slot] | forced
        elif slot == 4:
            present = jnp.ones((NTL, NTS), dtype=bool)
        else:
            mirror = 8 - slot
            forced_m = (rows == 1) & (cols == 1) | (rows + row_off == 1) & (cols + col_off == 1)
            present = jnp.roll(upper[:, :, mirror], (-row_off, -col_off), axis=(0, 1)) | forced_m
        columns.append(present & inside)
    mask = jnp.stack(columns, axis=-1)
    count = jnp.sum(mask.astype(jnp.int32), axis=-1).astype(jnp.int32)
    slots = jnp.arange(9, dtype=jnp.int32)
    order_key = jnp.where(mask, slots, slots + 9).astype(jnp.int32)
    ordered = jnp.argsort(order_key, axis=-1, stable=True).astype(jnp.int32)
    listing = jnp.where(slots < count[..., None], ordered, 4).astype(jnp.int32)
    return (listing, count)


def draw_block_list(key, part):
    return pattern_draw(key)[0]


def draw_block_count(key, part):
    return pattern_draw(key)[1]


def draw_edge_tiles(key, part):
    raw_key = jax.random.fold_in(key, 5)
    raw = 0.02 * jax.random.normal(raw_key, (NTL, NTS, 9, TILE, TILE), jnp.float32)
    tiles = []
    for slot in range(9):
        row_off = slot // 3 - 1
        col_off = slot % 3 - 1
        mirror = jnp.roll(raw[:, :, 8 - slot], (-row_off, -col_off), axis=(0, 1))
        tiles.append(raw[:, :, slot] + jnp.swapaxes(mirror, -1, -2))
    return jnp.stack(tiles, axis=2).astype(jnp.bfloat16)


def block_scale(key, shape, cuts, least, top_value):
    def one(axis_at, shards_of):
        draws = jax.random.uniform(jax.random.fold_in(jax.random.fold_in(key, 6), axis_at), (shards_of,), jnp.float32, least / len(cuts), top_value / len(cuts))
        return jnp.repeat(jnp.exp(draws), shape[axis_at] // shards_of).reshape((-1,) + (1,) * (len(shape) - axis_at - 1))

    loudness = one(*cuts[0])
    for cut in cuts[1:]:
        loudness = loudness * one(*cut)
    return loudness


def scatter_about(stream_key, dims, spread, most, cuts=(), kind=jnp.bfloat16):
    level = block_scale(stream_key, dims, cuts, -0.22, 0.18) if cuts else 1.0
    result = jax.random.normal(stream_key, dims, jnp.float32) * spread * level
    return jnp.minimum(jnp.maximum(result, -most), most).astype(kind)


def setup_inputs(seed: int = 0) -> dict:
    arg_keys = jax.random.split(jax.random.key(seed), 7)
    features = scatter_about(arg_keys[0], (NTL, NTS, TILE, F), 1.0, 6.0, ((0, 32), (1, 32)))
    weight = scatter_about(arg_keys[1], (F, F), F ** -0.5, 0.25)
    edge_tiles = draw_edge_tiles(jax.random.fold_in(arg_keys[6], 71), 0)
    block_list = draw_block_list(jax.random.fold_in(arg_keys[6], 71), 0)
    block_count = draw_block_count(jax.random.fold_in(arg_keys[6], 71), 0)
    grad_hidden = scatter_about(arg_keys[5], (NTL, NTS, TILE, F), 1.0, 6.0, ((0, 32), (1, 32)))
    return dict(features=features, weight=weight, edge_tiles=edge_tiles, block_list=block_list, block_count=block_count, grad_hidden=grad_hidden)


def slot_mask(block_list, block_count):
    slots = jnp.arange(9, dtype=jnp.int32)
    matches = block_list[..., :, None] == slots
    listed = slots[:, None] < block_count[..., None, None]
    return jnp.any(matches & listed, axis=-2)

def reference(features, weight, edge_tiles, block_list, block_count, grad_hidden):
    mask = slot_mask(block_list, block_count)
    effective = edge_tiles * mask[..., None, None].astype(jnp.bfloat16)
    tile_rows, tile_cols = (features.shape[0], features.shape[1])
    weight_f = weight.astype(jnp.float32)
    projected = jnp.einsum('abif,fg->abig', features.astype(jnp.float32), weight_f).astype(jnp.bfloat16)
    padded = jnp.pad(projected, ((1, 1), (1, 1), (0, 0), (0, 0)))
    summed = jnp.zeros(features.shape, jnp.float32)
    for row_off in range(3):
        for col_off in range(3):
            window = padded[row_off:row_off + tile_rows, col_off:col_off + tile_cols].astype(jnp.float32)
            tiles = effective[:, :, 3 * row_off + col_off].astype(jnp.float32)
            summed = summed + jnp.einsum('abij,abjf->abif', tiles, window)
    sigmoid_part = jax.nn.sigmoid(summed)
    hidden = (summed * sigmoid_part).astype(jnp.bfloat16)
    grad_pre = (grad_hidden.astype(jnp.float32) * sigmoid_part * (1.0 + summed * (1.0 - sigmoid_part))).astype(jnp.bfloat16)
    grad_f = grad_pre.astype(jnp.float32)
    pushed = jnp.zeros((tile_rows + 2, tile_cols + 2) + features.shape[2:], jnp.float32)
    for row_off in range(3):
        for col_off in range(3):
            tiles = effective[:, :, 3 * row_off + col_off].astype(jnp.float32)
            term = jnp.einsum('abji,abjf->abif', tiles, grad_f)
            pushed = pushed.at[row_off:row_off + tile_rows, col_off:col_off + tile_cols].add(term)
    back = pushed[1:-1, 1:-1].astype(jnp.bfloat16)
    back_f = back.astype(jnp.float32)
    grad_features = jnp.einsum('abig,fg->abif', back_f, weight_f).astype(jnp.bfloat16)
    grad_weight = jnp.einsum('abif,abig->fg', features.astype(jnp.float32), back_f) * (1.0 / math.sqrt(NODES))
    return (hidden, grad_features, grad_weight)
```

```python
import functools
import math

import jax
import jax.numpy as jnp
from jax import lax
from jax.experimental import pallas as pl
from jax.experimental.pallas import tpu as pltpu
from jax.sharding import PartitionSpec as P

MESH = pl.DeviceIdType.MESH
F32 = jnp.float32
BF16 = jnp.bfloat16
TILE = 128
NX, NY, NZ, NYLO = 8, 8, 8, 4
LOOP, SECTION = 2 * NX * (NY // NYLO), NYLO * NZ
DIRS = [(du, dv) for du in (-1, 0, 1) for dv in (-1, 0, 1) if (du, dv) != (0, 0)]


def dot(a, b):
    return jnp.dot(a, b, preferred_element_type=F32)


def dot_rows(a, b):
    return lax.dot_general(a, b, (((0,), (0,)), ((), ())), preferred_element_type=F32)


def dot_cols(a, b):
    return lax.dot_general(a, b, (((1,), (1,)), ((), ())), preferred_element_type=F32)


def kernel(
    blist,
    bcount,
    feat,
    weight,
    edge,
    gh,
    hid_o,
    gf_o,
    gw_o,
    w_v,
    e_v,
    gh_v,
    a_mid,
    a_side,
    acc,
    hid_v,
    gf_v,
    pc,
    ps,
    qc,
    qs,
    ax,
    axp,
    back,
    part,
    s1,
    r1,
    s2,
    r2,
    r3,
    t2,
    t1,
    tp,
    in_sem,
    out_sem,
    halo_ss,
    halo_rs,
    ghalo_ss,
    ghalo_rs,
    ax_sem,
    ar_ss,
    ar_rs,
    tp_ss,
    tp_rs,
):
    L = lax.axis_index("loop")
    S = lax.axis_index("section")
    core = lax.rem(L, 2)
    x = lax.rem(L // 2, NX)
    y = (L // (2 * NX)) * NYLO + S // NZ
    z = lax.rem(S, NZ)

    def place(px, py, pz):
        return ((py // NYLO) * (2 * NX) + px * 2 + core, lax.rem(py, NYLO) * NZ + pz)

    def peer(axis, d):
        if axis == "x":
            k = lax.rem(x + d, NX)
            return k, place(k, y, z)
        if axis == "y":
            k = lax.rem(y + d, NY)
            return k, place(x, k, z)
        k = lax.rem(z + d, NZ)
        return k, place(x, y, k)

    def inside(du, dv):
        ok = jnp.bool_(True)
        if du:
            ok = (L + du >= 0) & (L + du < LOOP)
        if dv:
            ok_v = (S + dv >= 0) & (S + dv < SECTION)
            ok = ok & ok_v if du else ok_v
        return ok

    barrier = pltpu.get_barrier_semaphore()
    for du, dv in DIRS:

        @pl.when(inside(du, dv))
        def _(du=du, dv=dv):
            pl.semaphore_signal(barrier, inc=1, device_id=(L + du, S + dv), device_id_type=MESH)

    for axis in "xyz":
        for d in range(1, 8):
            _, dev = peer(axis, d)
            pl.semaphore_signal(barrier, inc=1, device_id=dev, device_id_type=MESH)

    loads = [
        pltpu.make_async_copy(feat, pc.at[1], in_sem.at[0]),
        pltpu.make_async_copy(edge, e_v, in_sem.at[1]),
        pltpu.make_async_copy(weight, w_v, in_sem.at[2]),
        pltpu.make_async_copy(gh, gh_v, in_sem.at[3]),
    ]
    for load in loads:
        load.start()

    for mid, side in ((pc, ps), (qc, qs)):
        for du, u in ((-1, 0), (1, 2)):

            @pl.when(jnp.logical_not(inside(du, 0)))
            def _(mid=mid, side=side, u=u):
                mid[u] = jnp.zeros((2 * TILE, 512), BF16)
                for k in range(2):
                    side[k, pl.ds(u * TILE, TILE), :] = jnp.zeros((TILE, 512), BF16)

        for dv, k in ((-1, 0), (1, 1)):

            @pl.when(jnp.logical_not(inside(0, dv)))
            def _(side=side, k=k):
                side[k] = jnp.zeros((3 * TILE, 512), BF16)

    rows_in = (L > 0).astype(jnp.int32) + (L < LOOP - 1).astype(jnp.int32)
    cols_in = (S > 0).astype(jnp.int32) + (S < SECTION - 1).astype(jnp.int32)

    def halo_copy(mid, side, ss, rs, n):
        du, dv = DIRS[n]
        if dv == 0:
            src, dst = mid.at[1], mid.at[1 - du]
        elif dv == 1:
            src, dst = mid.at[1, pl.ds(TILE, TILE)], side.at[0, pl.ds((1 - du) * TILE, TILE)]
        else:
            src, dst = mid.at[1, pl.ds(0, TILE)], side.at[1, pl.ds((1 - du) * TILE, TILE)]
        return pltpu.make_async_remote_copy(
            src_ref=src,
            dst_ref=dst,
            send_sem=ss.at[n],
            recv_sem=rs.at[n],
            device_id=(L + du, S + dv),
            device_id_type=MESH,
        )

    def halo_start(mid, side, ss, rs, n, extra=None):
        du, dv = DIRS[n]
        ok = inside(du, dv)
        if extra is not None:
            ok = ok & extra

        @pl.when(ok)
        def _():
            halo_copy(mid, side, ss, rs, n).start()

    def halo_wait_recv(mid, side, ss, rs, n):
        du, dv = DIRS[n]

        @pl.when(inside(-du, -dv))
        def _():
            halo_copy(mid, side, ss, rs, n).wait_recv()

    def halo_wait_send(mid, side, ss, rs, n):
        du, dv = DIRS[n]

        @pl.when(inside(du, dv))
        def _():
            halo_copy(mid, side, ss, rs, n).wait_send()

    order = [DIRS.index(d) for d in ((-1, 0), (1, 0), (0, -1), (0, 1), (-1, -1), (-1, 1), (1, -1), (1, 1))]

    loads[0].wait()
    pl.semaphore_wait(barrier, 21 + rows_in + cols_in + rows_in * cols_in)
    for n in order:
        halo_start(pc, ps, halo_ss, halo_rs, n)

    loads[1].wait()
    for b in range(2):
        bits = jnp.int32(0)
        for k in range(9):
            bits = bits | jnp.where(k < bcount[0, b], jnp.int32(1) << blist[0, b, k], 0)
        for s in range(9):
            tile = jnp.where(((bits >> s) & 1) == 1, e_v[b, s], jnp.zeros((TILE, TILE), BF16))
            u, v = s // 3, s % 3
            col = b + v
            if col in (1, 2):
                a_mid[u, b * TILE : (b + 1) * TILE, (col - 1) * TILE : col * TILE] = tile
            else:
                a_side[b, :, u * TILE : (u + 1) * TILE] = tile

    def aggregate(mid, side, ss, rs):
        acc[...] = dot(a_mid[1], mid[1])
        for n in order[:2]:
            halo_wait_recv(mid, side, ss, rs, n)
        acc[...] += dot(a_mid[0], mid[0]) + dot(a_mid[2], mid[2])
        for n in order[2:]:
            halo_wait_recv(mid, side, ss, rs, n)
        for b in range(2):
            acc[b * TILE : (b + 1) * TILE] += dot(a_side[b], side[b])

    aggregate(pc, ps, halo_ss, halo_rs)
    for half in range(2):
        ax[half] = acc[:, half * 256 : (half + 1) * 256].astype(BF16)
    partner = (L + 1 - 2 * core, S)
    ax_copy = pltpu.make_async_remote_copy(
        src_ref=ax.at[1 - core],
        dst_ref=axp,
        send_sem=ax_sem.at[0],
        recv_sem=ax_sem.at[1],
        device_id=partner,
        device_id_type=MESH,
    )
    ax_copy.start()
    loads[2].wait()
    acc[...] = dot(ax[0], w_v[:256]) + dot(ax[1], w_v[256:])
    loads[3].wait()
    for r in range(0, 256, 32):
        p = acc[r : r + 32]
        sig = jax.nn.sigmoid(p)
        hid_v[r : r + 32] = (p * sig).astype(BF16)
        g = gh_v[r : r + 32].astype(F32)
        qc[1, r : r + 32] = (g * sig * (1.0 + p * (1.0 - sig))).astype(BF16)

    down, up = DIRS.index((-1, 0)), DIRS.index((1, 0))
    halo_start(qc, qs, ghalo_ss, ghalo_rs, up, core == 0)
    halo_start(qc, qs, ghalo_ss, ghalo_rs, down, core == 1)
    hid_out = pltpu.make_async_copy(hid_v, hid_o, out_sem.at[0])
    hid_out.start()

    own_part = dot_rows(ax[core], qc[1])
    part[...] = own_part.reshape(2, 8, 16, 512)
    ax_copy.wait()

    @pl.when(core == 0)
    def _():
        halo_wait_recv(qc, qs, ghalo_ss, ghalo_rs, down)

    @pl.when(core == 1)
    def _():
        halo_wait_recv(qc, qs, ghalo_ss, ghalo_rs, up)

    part[...] += dot_rows(axp[...], qc[2 * (1 - core)]).reshape(2, 8, 16, 512)
    s1[...] = part[...].astype(BF16)

    first = ("y", "x")
    second = ("x", "y")
    at = {"x": x, "y": y, "z": z}

    def ar(stage, h, d, src, dst, dev):
        k = (stage * 2 + h) * 7 + d - 1
        return pltpu.make_async_remote_copy(
            src_ref=src,
            dst_ref=dst,
            send_sem=ar_ss.at[k],
            recv_sem=ar_rs.at[k],
            device_id=dev,
            device_id_type=MESH,
        )

    sent = []
    both = [(h, d) for d in (4, 3, 5, 2, 6, 1, 7) for h in range(2)]

    def run(stage, make):
        copies = []
        for h, d in both:
            c = make(stage, h, d)
            c.start()
            copies.append(c)
        sent.extend(copies)
        return copies

    def make1(stage, h, d):
        k, dev = peer(first[h], d)
        return ar(stage, h, d, s1.at[h, k], r1.at[h, d - 1], dev)

    copies = run(0, make1)
    halo_start(qc, qs, ghalo_ss, ghalo_rs, up, core == 1)
    halo_start(qc, qs, ghalo_ss, ghalo_rs, down, core == 0)
    for n in order[2:]:
        halo_start(qc, qs, ghalo_ss, ghalo_rs, n)
    for c in copies:
        c.wait_recv()
    for h in range(2):
        total = part[h, at[first[h]]]
        for d in range(7):
            total = total + r1[h, d].astype(F32)
        for t in range(8):
            s2[h, t] = total[(t // 4) * 8 : (t // 4) * 8 + 8, (t % 4) * 128 : (t % 4) * 128 + 128]

    def make2(stage, h, d):
        k, dev = peer(second[h], d)
        return ar(stage, h, d, s2.at[h, k], r2.at[h, d - 1], dev)

    for c in run(1, make2):
        c.wait_recv()
    for h in range(2):
        total = s2[h, at[second[h]]]
        for d in range(7):
            total = total + r2[h, d]
        r3[h, z] = total

    def make3(stage, h, d):
        _, dev = peer("z", d)
        return ar(stage, h, d, r3.at[h, z], r3.at[h, z], dev)

    for c in run(2, make3):
        c.wait_recv()
    for h in range(2):
        total = r3[h, 0]
        for d in range(1, 8):
            total = total + r3[h, d]
        t2[h, at[second[h]]] = total

    def make4(stage, h, d):
        _, dev = peer(second[h], d)
        return ar(stage, h, d, t2.at[h, at[second[h]]], t2.at[h, at[second[h]]], dev)

    for c in run(3, make4):
        c.wait_recv()
    for h in range(2):
        lines = [jnp.concatenate([t2[h, 4 * r + k] for k in range(4)], axis=1) for r in range(2)]
        t1[h, at[first[h]]] = jnp.concatenate(lines, axis=0).astype(BF16)

    def make5(stage, h, d):
        _, dev = peer(first[h], d)
        return ar(stage, h, d, t1.at[h, at[first[h]]], t1.at[h, at[first[h]]], dev)

    copies = run(4, make5)

    aggregate_waited = [n for n in order]
    acc[...] = dot(a_mid[1], qc[1])
    for n in aggregate_waited:
        if n == down:

            @pl.when(core == 1)
            def _():
                halo_wait_recv(qc, qs, ghalo_ss, ghalo_rs, down)

        elif n == up:

            @pl.when(core == 0)
            def _():
                halo_wait_recv(qc, qs, ghalo_ss, ghalo_rs, up)

        else:
            halo_wait_recv(qc, qs, ghalo_ss, ghalo_rs, n)
    acc[...] += dot(a_mid[0], qc[0]) + dot(a_mid[2], qc[2])
    for b in range(2):
        acc[b * TILE : (b + 1) * TILE] += dot(a_side[b], qs[b])
    back[...] = acc[...].astype(BF16)
    gf_v[...] = dot_cols(back[...], w_v[...]).astype(BF16)
    gf_out = pltpu.make_async_copy(gf_v, gf_o, out_sem.at[1])
    gf_out.start()

    for c in copies:
        c.wait_recv()
    pair = pltpu.make_async_remote_copy(
        src_ref=t1,
        dst_ref=tp,
        send_sem=tp_ss,
        recv_sem=tp_rs,
        device_id=partner,
        device_id_type=MESH,
    )
    pair.start()
    own_out = pltpu.make_async_copy(t1, gw_o.at[core], out_sem.at[2])
    own_out.start()
    pair.wait_recv()
    other_out = pltpu.make_async_copy(tp, gw_o.at[1 - core], out_sem.at[3])
    other_out.start()

    for c in sent:
        c.wait_send()
    pair.wait_send()
    for n in order:
        halo_wait_send(pc, ps, halo_ss, halo_rs, n)
        halo_wait_send(qc, qs, ghalo_ss, ghalo_rs, n)
    hid_out.wait()
    gf_out.wait()
    own_out.wait()
    other_out.wait()


def per_device(features, weight, edge_tiles, block_list, block_count, grad_hidden):
    rows, width = 2 * TILE, features.shape[3]
    nodes = LOOP * SECTION * rows
    anywhere = pl.BlockSpec(memory_space=pl.ANY)
    scalars = pl.BlockSpec(memory_space=pltpu.SMEM)
    dma = pltpu.SemaphoreType.DMA
    vmem = pltpu.VMEM
    hidden, grad_features, total = pl.pallas_call(
        kernel,
        out_shape=[
            jax.ShapeDtypeStruct((rows, width), BF16),
            jax.ShapeDtypeStruct((rows, width), BF16),
            jax.ShapeDtypeStruct((2, 2, 8, 16, width), BF16),
        ],
        in_specs=[scalars, scalars, anywhere, anywhere, anywhere, anywhere],
        out_specs=[anywhere] * 3,
        scratch_shapes=[
            vmem((width, width), BF16),
            vmem((2, 9, TILE, TILE), BF16),
            vmem((rows, width), BF16),
            vmem((3, rows, rows), BF16),
            vmem((2, TILE, 3 * TILE), BF16),
            vmem((rows, width), F32),
            vmem((rows, width), BF16),
            vmem((rows, width), BF16),
            vmem((3, rows, width), BF16),
            vmem((2, 3 * TILE, width), BF16),
            vmem((3, rows, width), BF16),
            vmem((2, 3 * TILE, width), BF16),
            vmem((2, rows, 256), BF16),
            vmem((rows, 256), BF16),
            vmem((rows, width), BF16),
            vmem((2, 8, 16, width), F32),
            vmem((2, 8, 16, width), BF16),
            vmem((2, 7, 16, width), BF16),
            vmem((2, 8, 8, 128), F32),
            vmem((2, 7, 8, 128), F32),
            vmem((2, 8, 8, 128), F32),
            vmem((2, 8, 8, 128), F32),
            vmem((2, 8, 16, width), BF16),
            vmem((2, 8, 16, width), BF16),
            dma((4,)),
            dma((4,)),
            dma((8,)),
            dma((8,)),
            dma((8,)),
            dma((8,)),
            dma((2,)),
            dma((70,)),
            dma((70,)),
            dma,
            dma,
        ],
        compiler_params=pltpu.CompilerParams(collective_id=0, has_side_effects=True),
    )(
        block_list,
        block_count,
        features.reshape(rows, width),
        weight,
        edge_tiles.reshape(2, 9, TILE, TILE),
        grad_hidden.reshape(rows, width),
    )
    grad_weight = total.reshape(width, width).astype(F32) * (1.0 / math.sqrt(nodes))
    return (hidden.reshape(features.shape), grad_features.reshape(features.shape), grad_weight)


def solution(mesh):
    placed = (
        P("loop", "section", None, None),
        P(),
        P("loop", "section", None, None, None),
        P("loop", "section", None),
        P("loop", "section"),
        P("loop", "section", None, None),
    )
    return jax.shard_map(
        per_device,
        mesh=mesh,
        in_specs=placed,
        out_specs=(P("loop", "section", None, None), P("loop", "section", None, None), P()),
        check_vma=False,
    )
```

```python
import functools
import math

import jax
import jax.numpy as jnp
from jax import lax
from jax.experimental import pallas as pl
from jax.experimental.pallas import tpu as pltpu
from jax.sharding import PartitionSpec as P

MESH = pl.DeviceIdType.MESH
F32 = jnp.float32
BF16 = jnp.bfloat16
TILE = 128
NX, NY, NZ, NYLO = 8, 8, 8, 4
LOOP, SECTION = 2 * NX * (NY // NYLO), NYLO * NZ


def dot(a, b):
    return jnp.dot(a, b, preferred_element_type=F32)


def dot_rows(a, b):
    return lax.dot_general(a, b, (((0,), (0,)), ((), ())), preferred_element_type=F32)


def dot_cols(a, b):
    return lax.dot_general(a, b, (((1,), (1,)), ((), ())), preferred_element_type=F32)


def kernel(
    scale,
    blist,
    bcount,
    feat,
    weight,
    edge,
    gh,
    hid_v,
    gf_v,
    gw_v,
    w_v,
    e_v,
    gh_v,
    a_mid,
    a_side,
    acc,
    pc,
    ps,
    qc,
    qs,
    ax,
    axp,
    back,
    part,
    s1,
    r1,
    s2,
    r2,
    r3,
    t2,
    t1,
    tp,
    in_sem,
    halo_ss,
    halo_rs,
    ghalo_ss,
    ghalo_rs,
    ax_sem,
    ar_ss,
    ar_rs,
    tp_ss,
    tp_rs,
):
    L = lax.axis_index("loop")
    S = lax.axis_index("section")
    core = lax.rem(L, 2)
    x = lax.rem(L // 2, NX)
    y = (L // (2 * NX)) * NYLO + S // NZ
    z = lax.rem(S, NZ)

    def place(px, py, pz):
        return ((py // NYLO) * (2 * NX) + px * 2 + core, lax.rem(py, NYLO) * NZ + pz)

    def peer(axis, d):
        if axis == "x":
            k = lax.rem(x + d, NX)
            return k, place(k, y, z)
        if axis == "y":
            k = lax.rem(y + d, NY)
            return k, place(x, k, z)
        k = lax.rem(z + d, NZ)
        return k, place(x, y, k)

    out_row = L - 1 + 2 * core
    partner = (L + 1 - 2 * core, S)
    has_out = (out_row >= 0) & (out_row < LOOP)
    has_side = {-1: S > 0, 1: S < SECTION - 1}
    u_out, u_in = 2 * core, 2 * (1 - core)

    barrier = pltpu.get_barrier_semaphore()
    pl.semaphore_signal(barrier, inc=1, device_id=partner, device_id_type=MESH)

    @pl.when(has_out)
    def _():
        pl.semaphore_signal(barrier, inc=1, device_id=(out_row, S), device_id_type=MESH)

    for dv in (-1, 1):

        @pl.when(has_side[dv])
        def _(dv=dv):
            pl.semaphore_signal(barrier, inc=1, device_id=(L, S + dv), device_id_type=MESH)

    for axis in "xyz":
        for d in range(1, 8):
            _, dev = peer(axis, d)
            pl.semaphore_signal(barrier, inc=1, device_id=dev, device_id_type=MESH)

    loads = [
        pltpu.make_async_copy(feat, pc.at[1], in_sem.at[0]),
        pltpu.make_async_copy(edge, e_v, in_sem.at[1]),
        pltpu.make_async_copy(weight, w_v, in_sem.at[2]),
        pltpu.make_async_copy(gh, gh_v, in_sem.at[3]),
    ]
    for load in loads:
        load.start()

    for mid, side in ((pc, ps), (qc, qs)):

        @pl.when(jnp.logical_not(has_out))
        def _(mid=mid, side=side):
            mid[u_out] = jnp.zeros((2 * TILE, 512), BF16)
            for k in range(2):
                side[k, u_out] = jnp.zeros((TILE, 512), BF16)

        for dv, k in ((-1, 0), (1, 1)):

            @pl.when(jnp.logical_not(has_side[dv]))
            def _(side=side, k=k):
                side[k] = jnp.zeros((3, TILE, 512), BF16)

    def halo(mid, side, ss, rs):
        def copy(n, src, dst, dev):
            return pltpu.make_async_remote_copy(
                src_ref=src,
                dst_ref=dst,
                send_sem=ss.at[n],
                recv_sem=rs.at[n],
                device_id=dev,
                device_id_type=MESH,
            )

        cut = {-1: pl.ds(0, TILE), 1: pl.ds(TILE, TILE)}
        slot = {-1: 1, 1: 0}
        jobs = {
            "partner": (copy(0, mid.at[1], mid.at[u_out], partner), None, None),
            "outer": (copy(1, mid.at[1], mid.at[u_in], (out_row, S)), has_out, has_out),
        }
        for i, dv in enumerate((-1, 1)):
            dev = (L, S + dv)
            jobs["side", dv] = (
                copy(2 + i, mid.at[1, cut[dv]], side.at[slot[dv], 1], dev),
                has_side[dv],
                has_side[-dv],
            )
            jobs["relay", dv] = (
                copy(4 + i, mid.at[u_out, cut[dv]], side.at[slot[dv], u_out], dev),
                has_side[dv] & has_out,
                has_side[-dv] & has_out,
            )
            jobs["share", dv] = (
                copy(6 + i, side.at[slot[dv], 1], side.at[slot[dv], u_out], partner),
                has_side[-dv],
                has_side[-dv],
            )

        def start(*keys):
            for key in keys:
                job, sends, _ = jobs[key]
                job.start() if sends is None else pl.when(sends)(job.start)

        def arrived(*keys):
            for key in keys:
                job, _, gets = jobs[key]
                job.wait_recv() if gets is None else pl.when(gets)(job.wait_recv)

        def drained():
            for job, sends, _ in jobs.values():
                job.wait_send() if sends is None else pl.when(sends)(job.wait_send)

        return start, arrived, drained

    p_start, p_arrived, p_drained = halo(pc, ps, halo_ss, halo_rs)
    q_start, q_arrived, q_drained = halo(qc, qs, ghalo_ss, ghalo_rs)
    sides = (("side", -1), ("side", 1))
    relays = (("relay", -1), ("relay", 1))
    shares = (("share", -1), ("share", 1))

    loads[0].wait()
    greeted = has_out.astype(jnp.int32) + sum(has_side[dv].astype(jnp.int32) for dv in (-1, 1))
    pl.semaphore_wait(barrier, 22 + greeted)
    p_start("outer", *sides, "partner")

    loads[1].wait()
    for b in range(2):
        bits = jnp.int32(0)
        for k in range(9):
            bits = bits | jnp.where(k < bcount[0, b], jnp.int32(1) << blist[0, b, k], 0)
        for s in range(9):
            tile = jnp.where(((bits >> s) & 1) == 1, e_v[b, s], jnp.zeros((TILE, TILE), BF16))
            u, v = s // 3, s % 3
            col = b + v
            if col in (1, 2):
                a_mid[u, b * TILE : (b + 1) * TILE, (col - 1) * TILE : col * TILE] = tile
            else:
                a_side[b, u] = tile

    def add_sides(side):
        for b in range(2):
            acc[b * TILE : (b + 1) * TILE] += sum(dot(a_side[b, u], side[b, u]) for u in range(3))

    acc[...] = dot(a_mid[1], pc[1])
    p_arrived("partner")
    acc[...] += dot(a_mid[u_in], pc[u_in])
    for dv in (-1, 1):
        p_arrived(("side", dv))
        p_start(("share", dv))
    p_arrived("outer")
    p_start(*relays)
    acc[...] += dot(a_mid[u_out], pc[u_out])
    p_arrived(*shares, *relays)
    add_sides(ps)

    for half in range(2):
        ax[half] = acc[:, half * 256 : (half + 1) * 256].astype(BF16)
    ax_copy = pltpu.make_async_remote_copy(
        src_ref=ax.at[1 - core],
        dst_ref=axp,
        send_sem=ax_sem.at[0],
        recv_sem=ax_sem.at[1],
        device_id=partner,
        device_id_type=MESH,
    )
    ax_copy.start()
    loads[2].wait()
    acc[...] = dot(ax[0], w_v[:256]) + dot(ax[1], w_v[256:])
    loads[3].wait()
    for r in range(0, 256, 32):
        p = acc[r : r + 32]
        sig = jax.nn.sigmoid(p)
        hid_v[r : r + 32] = (p * sig).astype(BF16)
        g = gh_v[r : r + 32].astype(F32)
        qc[1, r : r + 32] = (g * sig * (1.0 + p * (1.0 - sig))).astype(BF16)

    q_start("partner")

    own_part = dot_rows(ax[core], qc[1])
    part[...] = own_part.reshape(2, 8, 16, 512)
    ax_copy.wait()

    q_arrived("partner")
    part[...] += dot_rows(axp[...], qc[u_in]).reshape(2, 8, 16, 512)
    s1[...] = part[...].astype(BF16)

    first = ("y", "x")
    second = ("x", "y")
    at = {"x": x, "y": y, "z": z}

    def ar(stage, h, d, src, dst, dev):
        k = (stage * 2 + h) * 7 + d - 1
        return pltpu.make_async_remote_copy(
            src_ref=src,
            dst_ref=dst,
            send_sem=ar_ss.at[k],
            recv_sem=ar_rs.at[k],
            device_id=dev,
            device_id_type=MESH,
        )

    sent = []
    both = [(h, d) for d in (4, 3, 5, 2, 6, 1, 7) for h in range(2)]

    def run(stage, make):
        copies = []
        for h, d in both:
            c = make(stage, h, d)
            c.start()
            copies.append(c)
        sent.extend(copies)
        return copies

    def make1(stage, h, d):
        k, dev = peer(first[h], d)
        return ar(stage, h, d, s1.at[h, k], r1.at[h, d - 1], dev)

    copies = run(0, make1)
    q_start("outer", *sides)
    for c in copies:
        c.wait_recv()
    for h in range(2):
        total = part[h, at[first[h]]]
        for d in range(7):
            total = total + r1[h, d].astype(F32)
        for t in range(8):
            s2[h, t] = total[(t // 4) * 8 : (t // 4) * 8 + 8, (t % 4) * 128 : (t % 4) * 128 + 128]

    def make2(stage, h, d):
        k, dev = peer(second[h], d)
        return ar(stage, h, d, s2.at[h, k], r2.at[h, d - 1], dev)

    for c in run(1, make2):
        c.wait_recv()
    for h in range(2):
        total = s2[h, at[second[h]]]
        for d in range(7):
            total = total + r2[h, d]
        r3[h, z] = total

    def make3(stage, h, d):
        _, dev = peer("z", d)
        return ar(stage, h, d, r3.at[h, z], r3.at[h, z], dev)

    copies = run(2, make3)
    for dv in (-1, 1):
        q_arrived(("side", dv))
        q_start(("share", dv))
    q_arrived("outer")
    q_start(*relays)
    for c in copies:
        c.wait_recv()
    for h in range(2):
        total = r3[h, 0]
        for d in range(1, 8):
            total = total + r3[h, d]
        t2[h, at[second[h]]] = total

    def make4(stage, h, d):
        _, dev = peer(second[h], d)
        return ar(stage, h, d, t2.at[h, at[second[h]]], t2.at[h, at[second[h]]], dev)

    for c in run(3, make4):
        c.wait_recv()
    for h in range(2):
        lines = [jnp.concatenate([t2[h, 4 * r + k] for k in range(4)], axis=1) for r in range(2)]
        t1[h, at[first[h]]] = jnp.concatenate(lines, axis=0).astype(BF16)

    def make5(stage, h, d):
        _, dev = peer(first[h], d)
        return ar(stage, h, d, t1.at[h, at[first[h]]], t1.at[h, at[first[h]]], dev)

    copies = run(4, make5)

    def pair(h, d):
        k = lax.rem(at[first[h]] + (8 - d), 8)
        c = pltpu.make_async_remote_copy(
            src_ref=t1.at[h, k],
            dst_ref=tp.at[h, k],
            send_sem=tp_ss.at[h * 8 + d],
            recv_sem=tp_rs.at[h * 8 + d],
            device_id=partner,
            device_id_type=MESH,
        )
        c.start()
        return c

    pairs = [pair(h, 0) for h in range(2)]

    acc[...] = dot(a_mid[0], qc[0]) + dot(a_mid[1], qc[1]) + dot(a_mid[2], qc[2])
    q_arrived(*shares, *relays)
    add_sides(qs)
    back[...] = acc[...].astype(BF16)
    gf_v[...] = dot_cols(back[...], w_v[...]).astype(BF16)

    for (h, d), c in sorted(zip(both, copies), key=lambda e: (min(e[0][1], 8 - e[0][1]), e[0])):
        c.wait_recv()
        pairs.append(pair(h, d))
    gw_v[core] = t1[...].astype(F32) * scale
    for c in pairs:
        c.wait_recv()
    gw_v[1 - core] = tp[...].astype(F32) * scale

    for c in sent + pairs:
        c.wait_send()
    p_drained()
    q_drained()


def write_out(hid_v, gf_v, gw_v, hid_o, gf_o, gw_o, sem):
    copies = [
        pltpu.make_async_copy(gw_v, gw_o, sem.at[0]),
        pltpu.make_async_copy(hid_v, hid_o, sem.at[1]),
        pltpu.make_async_copy(gf_v, gf_o, sem.at[2]),
    ]
    for copy in copies:
        copy.start()
    for copy in copies:
        copy.wait()


def per_device(features, weight, edge_tiles, block_list, block_count, grad_hidden):
    rows, width = 2 * TILE, features.shape[3]
    nodes = LOOP * SECTION * rows
    local = pl.BlockSpec(memory_space=pltpu.VMEM)
    anywhere = pl.BlockSpec(memory_space=pl.ANY)
    scalars = pl.BlockSpec(memory_space=pltpu.SMEM)
    dma = pltpu.SemaphoreType.DMA
    vmem = pltpu.VMEM
    results = pl.pallas_call(
        functools.partial(kernel, 1.0 / math.sqrt(nodes)),
        out_shape=[
            pltpu.VMEM((rows, width), BF16),
            pltpu.VMEM((rows, width), BF16),
            pltpu.VMEM((2, 2, 8, 16, width), F32),
        ],
        in_specs=[scalars, scalars, anywhere, anywhere, anywhere, anywhere],
        out_specs=[local] * 3,
        scratch_shapes=[
            vmem((width, width), BF16),
            vmem((2, 9, TILE, TILE), BF16),
            vmem((rows, width), BF16),
            vmem((3, rows, rows), BF16),
            vmem((2, 3, TILE, TILE), BF16),
            vmem((rows, width), F32),
            vmem((3, rows, width), BF16),
            vmem((2, 3, TILE, width), BF16),
            vmem((3, rows, width), BF16),
            vmem((2, 3, TILE, width), BF16),
            vmem((2, rows, 256), BF16),
            vmem((rows, 256), BF16),
            vmem((rows, width), BF16),
            vmem((2, 8, 16, width), F32),
            vmem((2, 8, 16, width), BF16),
            vmem((2, 7, 16, width), BF16),
            vmem((2, 8, 8, 128), F32),
            vmem((2, 7, 8, 128), F32),
            vmem((2, 8, 8, 128), F32),
            vmem((2, 8, 8, 128), F32),
            vmem((2, 8, 16, width), BF16),
            vmem((2, 8, 16, width), BF16),
            dma((4,)),
            dma((8,)),
            dma((8,)),
            dma((8,)),
            dma((8,)),
            dma((2,)),
            dma((70,)),
            dma((70,)),
            dma((16,)),
            dma((16,)),
        ],
        compiler_params=pltpu.CompilerParams(collective_id=0, has_side_effects=True),
    )(
        block_list,
        block_count,
        features.reshape(rows, width),
        weight,
        edge_tiles.reshape(2, 9, TILE, TILE),
        grad_hidden.reshape(rows, width),
    )
    hidden, grad_features, grad_weight = pl.pallas_call(
        write_out,
        out_shape=[
            jax.ShapeDtypeStruct((rows, width), BF16),
            jax.ShapeDtypeStruct((rows, width), BF16),
            jax.ShapeDtypeStruct((2, 2, 8, 16, width), F32),
        ],
        in_specs=[local] * 3,
        out_specs=[anywhere] * 3,
        scratch_shapes=[dma((3,))],
    )(*[pltpu.with_memory_space_constraint(r, pltpu.VMEM) for r in results])
    grad_weight = grad_weight.reshape(width, width)
    return (hidden.reshape(features.shape), grad_features.reshape(features.shape), grad_weight)


def solution(mesh):
    placed = (
        P("loop", "section", None, None),
        P(),
        P("loop", "section", None, None, None),
        P("loop", "section", None),
        P("loop", "section"),
        P("loop", "section", None, None),
    )
    return jax.shard_map(
        per_device,
        mesh=mesh,
        in_specs=placed,
        out_specs=(P("loop", "section", None, None), P("loop", "section", None, None), P()),
        check_vma=False,
    )
```

```python
import functools
import math

import jax
import jax.numpy as jnp
from jax import lax
from jax.experimental import pallas as pl
from jax.experimental.pallas import tpu as pltpu
from jax.sharding import PartitionSpec as P

MESH = pl.DeviceIdType.MESH
F32 = jnp.float32
BF16 = jnp.bfloat16
TILE = 128
NX, NY, NZ, NYLO = 8, 8, 8, 4
LOOP, SECTION = 2 * NX * (NY // NYLO), NYLO * NZ


def dot(a, b):
    return jnp.dot(a, b, preferred_element_type=F32)


def dot_rows(a, b):
    return lax.dot_general(a, b, (((0,), (0,)), ((), ())), preferred_element_type=F32)


def dot_cols(a, b):
    return lax.dot_general(a, b, (((1,), (1,)), ((), ())), preferred_element_type=F32)


def kernel(
    scale,
    blist,
    bcount,
    feat,
    weight,
    edge,
    gh,
    hid_v,
    gf_v,
    gw_v,
    w_v,
    e_v,
    gh_v,
    a_mid,
    a_side,
    acc,
    pc,
    ps,
    qc,
    qs,
    ax,
    axp,
    back,
    part,
    s1,
    r1,
    s2,
    r2,
    r3,
    t2,
    t1,
    tp,
    in_sem,
    halo_ss,
    halo_rs,
    ghalo_ss,
    ghalo_rs,
    ax_sem,
    ar_ss,
    ar_rs,
    tp_ss,
    tp_rs,
    entered,
):
    L = lax.axis_index("loop")
    S = lax.axis_index("section")
    core = lax.rem(L, 2)
    x = lax.rem(L // 2, NX)
    y = (L // (2 * NX)) * NYLO + S // NZ
    z = lax.rem(S, NZ)

    def place(px, py, pz):
        return ((py // NYLO) * (2 * NX) + px * 2 + core, lax.rem(py, NYLO) * NZ + pz)

    def peer(axis, d):
        if axis == "x":
            k = lax.rem(x + d, NX)
            return k, place(k, y, z)
        if axis == "y":
            k = lax.rem(y + d, NY)
            return k, place(x, k, z)
        k = lax.rem(z + d, NZ)
        return k, place(x, y, k)

    out_row = L - 1 + 2 * core
    partner = (L + 1 - 2 * core, S)
    has_out = (out_row >= 0) & (out_row < LOOP)
    has_side = {-1: S > 0, 1: S < SECTION - 1}
    u_out, u_in = 2 * core, 2 * (1 - core)

    barrier = pltpu.get_barrier_semaphore()
    pl.semaphore_signal(barrier, inc=1, device_id=partner, device_id_type=MESH)

    @pl.when(has_out)
    def _():
        pl.semaphore_signal(barrier, inc=1, device_id=(out_row, S), device_id_type=MESH)

    for dv in (-1, 1):

        @pl.when(has_side[dv])
        def _(dv=dv):
            pl.semaphore_signal(barrier, inc=1, device_id=(L, S + dv), device_id_type=MESH)

    def tell(sem, axes, hops):
        for axis in axes:
            for d in (hops, 8 - hops):
                pl.semaphore_signal(sem, inc=1, device_id=peer(axis, d)[1], device_id_type=MESH)

    tell(barrier, "xyz", 1)

    loads = [
        pltpu.make_async_copy(feat, pc.at[1], in_sem.at[0]),
        pltpu.make_async_copy(edge, e_v, in_sem.at[1]),
        pltpu.make_async_copy(weight, w_v, in_sem.at[2]),
        pltpu.make_async_copy(gh, gh_v, in_sem.at[3]),
    ]
    for load in loads:
        load.start()

    for mid, side in ((pc, ps), (qc, qs)):

        @pl.when(jnp.logical_not(has_out))
        def _(mid=mid, side=side):
            mid[u_out] = jnp.zeros((2 * TILE, 512), BF16)
            for k in range(2):
                side[k, u_out] = jnp.zeros((TILE, 512), BF16)

        for dv, k in ((-1, 0), (1, 1)):

            @pl.when(jnp.logical_not(has_side[dv]))
            def _(side=side, k=k):
                side[k] = jnp.zeros((3, TILE, 512), BF16)

    def halo(mid, side, ss, rs):
        def copy(n, src, dst, dev):
            return pltpu.make_async_remote_copy(
                src_ref=src,
                dst_ref=dst,
                send_sem=ss.at[n],
                recv_sem=rs.at[n],
                device_id=dev,
                device_id_type=MESH,
            )

        cut = {-1: pl.ds(0, TILE), 1: pl.ds(TILE, TILE)}
        slot = {-1: 1, 1: 0}
        jobs = {
            "partner": (copy(0, mid.at[1], mid.at[u_out], partner), None, None),
        }
        for i, dv in enumerate((-1, 1)):
            dev = (L, S + dv)
            jobs["outer", dv] = (
                copy((1, 8)[i], mid.at[1, cut[dv]], mid.at[u_in, cut[dv]], (out_row, S)),
                has_out,
                has_out,
            )
            jobs["side", dv] = (
                copy(2 + i, mid.at[1, cut[dv]], side.at[slot[dv], 1], dev),
                has_side[dv],
                has_side[-dv],
            )
            jobs["relay", dv] = (
                copy(4 + i, mid.at[u_out, cut[dv]], side.at[slot[dv], u_out], dev),
                has_side[dv] & has_out,
                has_side[-dv] & has_out,
            )
            jobs["share", dv] = (
                copy(6 + i, side.at[slot[dv], 1], side.at[slot[dv], u_out], partner),
                has_side[-dv],
                has_side[-dv],
            )

        def start(*keys):
            for key in keys:
                job, sends, _ = jobs[key]
                job.start() if sends is None else pl.when(sends)(job.start)

        def arrived(*keys):
            for key in keys:
                job, _, gets = jobs[key]
                job.wait_recv() if gets is None else pl.when(gets)(job.wait_recv)

        def drained():
            for job, sends, _ in jobs.values():
                job.wait_send() if sends is None else pl.when(sends)(job.wait_send)

        return start, arrived, drained

    p_start, p_arrived, p_drained = halo(pc, ps, halo_ss, halo_rs)
    q_start, q_arrived, q_drained = halo(qc, qs, ghalo_ss, ghalo_rs)
    sides = (("side", -1), ("side", 1))
    relays = (("relay", -1), ("relay", 1))
    shares = (("share", -1), ("share", 1))
    outers = (("outer", -1), ("outer", 1))

    loads[0].wait()
    greeted = has_out.astype(jnp.int32) + sum(has_side[dv].astype(jnp.int32) for dv in (-1, 1))
    pl.semaphore_wait(barrier, 7 + greeted)
    p_start(*outers, *sides, "partner")
    tell(entered.at[0], "xy", 1)
    tell(entered.at[1], "z", 1)

    loads[1].wait()
    for b in range(2):
        bits = jnp.int32(0)
        for k in range(9):
            bits = bits | jnp.where(k < bcount[0, b], jnp.int32(1) << blist[0, b, k], 0)
        for s in range(9):
            tile = jnp.where(((bits >> s) & 1) == 1, e_v[b, s], jnp.zeros((TILE, TILE), BF16))
            u, v = s // 3, s % 3
            col = b + v
            if col in (1, 2):
                a_mid[u, b * TILE : (b + 1) * TILE, (col - 1) * TILE : col * TILE] = tile
            else:
                a_side[b, u] = tile

    def add_sides(side):
        for b in range(2):
            acc[b * TILE : (b + 1) * TILE] += sum(dot(a_side[b, u], side[b, u]) for u in range(3))

    acc[...] = dot(a_mid[1], pc[1])
    p_arrived("partner")
    acc[...] += dot(a_mid[u_in], pc[u_in])
    for dv in (-1, 1):
        p_arrived(("side", dv))
        p_start(("share", dv))
    for dv in (-1, 1):
        p_arrived(("outer", dv))
        p_start(("relay", dv))
    pl.semaphore_wait(entered.at[0], 4)
    tell(entered.at[2], "xy", 2)
    pl.semaphore_wait(entered.at[1], 2)
    tell(entered.at[3], "z", 2)
    acc[...] += dot(a_mid[u_out], pc[u_out])
    p_arrived(*shares, *relays)
    add_sides(ps)

    for half in range(2):
        ax[half] = acc[:, half * 256 : (half + 1) * 256].astype(BF16)
    ax_copy = pltpu.make_async_remote_copy(
        src_ref=ax.at[1 - core],
        dst_ref=axp,
        send_sem=ax_sem.at[0],
        recv_sem=ax_sem.at[1],
        device_id=partner,
        device_id_type=MESH,
    )
    ax_copy.start()
    loads[2].wait()
    acc[...] = dot(ax[0], w_v[:256]) + dot(ax[1], w_v[256:])
    loads[3].wait()
    for r in range(0, 256, 32):
        p = acc[r : r + 32]
        sig = jax.nn.sigmoid(p)
        hid_v[r : r + 32] = (p * sig).astype(BF16)
        g = gh_v[r : r + 32].astype(F32)
        qc[1, r : r + 32] = (g * sig * (1.0 + p * (1.0 - sig))).astype(BF16)

    q_start("partner")

    own_part = dot_rows(ax[core], qc[1])
    part[...] = own_part.reshape(2, 8, 16, 512)
    ax_copy.wait()

    q_arrived("partner")
    part[...] += dot_rows(axp[...], qc[u_in]).reshape(2, 8, 16, 512)
    s1[...] = part[...].astype(BF16)

    first = ("y", "x")
    second = ("x", "y")
    at = {"x": x, "y": y, "z": z}

    def ar(stage, h, d, src, dst, dev):
        k = (stage * 2 + h) * 7 + d - 1
        return pltpu.make_async_remote_copy(
            src_ref=src,
            dst_ref=dst,
            send_sem=ar_ss.at[k],
            recv_sem=ar_rs.at[k],
            device_id=dev,
            device_id_type=MESH,
        )

    sent = []
    both = [(h, d) for d in (4, 3, 5, 2, 6, 1, 7) for h in range(2)]

    def run(stage, make):
        copies = []
        for h, d in both:
            c = make(stage, h, d)
            c.start()
            copies.append(c)
        sent.extend(copies)
        return copies

    def make1(stage, h, d):
        k, dev = peer(first[h], d)
        return ar(stage, h, d, s1.at[h, k], r1.at[h, d - 1], dev)

    pl.semaphore_wait(entered.at[2], 4)
    copies = run(0, make1)
    q_start(*outers, *sides)
    for c in copies:
        c.wait_recv()
    for h in range(2):
        total = part[h, at[first[h]]]
        for d in range(7):
            total = total + r1[h, d].astype(F32)
        for t in range(8):
            s2[h, t] = total[(t // 4) * 8 : (t // 4) * 8 + 8, (t % 4) * 128 : (t % 4) * 128 + 128]

    def make2(stage, h, d):
        k, dev = peer(second[h], d)
        return ar(stage, h, d, s2.at[h, k], r2.at[h, d - 1], dev)

    for c in run(1, make2):
        c.wait_recv()
    for h in range(2):
        total = s2[h, at[second[h]]]
        for d in range(7):
            total = total + r2[h, d]
        r3[h, z] = total

    def make3(stage, h, d):
        _, dev = peer("z", d)
        return ar(stage, h, d, r3.at[h, z], r3.at[h, z], dev)

    pl.semaphore_wait(entered.at[3], 2)
    copies = run(2, make3)
    for dv in (-1, 1):
        q_arrived(("side", dv))
        q_start(("share", dv))
    for c in copies:
        c.wait_recv()
    for h in range(2):
        total = r3[h, 0]
        for d in range(1, 8):
            total = total + r3[h, d]
        t2[h, at[second[h]]] = total

    def make4(stage, h, d):
        _, dev = peer(second[h], d)
        return ar(stage, h, d, t2.at[h, at[second[h]]], t2.at[h, at[second[h]]], dev)

    copies = run(3, make4)
    for dv in (-1, 1):
        q_arrived(("outer", dv))
        q_start(("relay", dv))
    acc[...] = dot(a_mid[0], qc[0]) + dot(a_mid[1], qc[1]) + dot(a_mid[2], qc[2])
    for c in copies:
        c.wait_recv()
    for h in range(2):
        lines = [jnp.concatenate([t2[h, 4 * r + k] for k in range(4)], axis=1) for r in range(2)]
        t1[h, at[first[h]]] = jnp.concatenate(lines, axis=0).astype(BF16)

    def make5(stage, h, d):
        _, dev = peer(first[h], d)
        return ar(stage, h, d, t1.at[h, at[first[h]]], t1.at[h, at[first[h]]], dev)

    copies = run(4, make5)

    def pair(h, d):
        k = lax.rem(at[first[h]] + (8 - d), 8)
        c = pltpu.make_async_remote_copy(
            src_ref=t1.at[h, k],
            dst_ref=tp.at[h, k],
            send_sem=tp_ss.at[h * 8 + d],
            recv_sem=tp_rs.at[h * 8 + d],
            device_id=partner,
            device_id_type=MESH,
        )
        c.start()
        return c

    pairs = [pair(h, 0) for h in range(2)]

    q_arrived(*shares, *relays)
    add_sides(qs)
    back[...] = acc[...].astype(BF16)
    gf_v[...] = dot_cols(back[...], w_v[...]).astype(BF16)

    for (h, d), c in sorted(zip(both, copies), key=lambda e: (min(e[0][1], 8 - e[0][1]), e[0])):
        c.wait_recv()
        pairs.append(pair(h, d))
    gw_v[core] = t1[...].astype(F32) * scale
    for c in pairs:
        c.wait_recv()
    gw_v[1 - core] = tp[...].astype(F32) * scale

    for c in sent + pairs:
        c.wait_send()
    p_drained()
    q_drained()


def write_out(hid_v, gf_v, gw_v, hid_o, gf_o, gw_o, sem):
    copies = [
        pltpu.make_async_copy(gw_v, gw_o, sem.at[0]),
        pltpu.make_async_copy(hid_v, hid_o, sem.at[1]),
        pltpu.make_async_copy(gf_v, gf_o, sem.at[2]),
    ]
    for copy in copies:
        copy.start()
    for copy in copies:
        copy.wait()


def per_device(features, weight, edge_tiles, block_list, block_count, grad_hidden):
    rows, width = 2 * TILE, features.shape[3]
    nodes = LOOP * SECTION * rows
    local = pl.BlockSpec(memory_space=pltpu.VMEM)
    anywhere = pl.BlockSpec(memory_space=pl.ANY)
    scalars = pl.BlockSpec(memory_space=pltpu.SMEM)
    dma = pltpu.SemaphoreType.DMA
    vmem = pltpu.VMEM
    results = pl.pallas_call(
        functools.partial(kernel, 1.0 / math.sqrt(nodes)),
        out_shape=[
            pltpu.VMEM((rows, width), BF16),
            pltpu.VMEM((rows, width), BF16),
            pltpu.VMEM((2, 2, 8, 16, width), F32),
        ],
        in_specs=[scalars, scalars, anywhere, anywhere, anywhere, anywhere],
        out_specs=[local] * 3,
        scratch_shapes=[
            vmem((width, width), BF16),
            vmem((2, 9, TILE, TILE), BF16),
            vmem((rows, width), BF16),
            vmem((3, rows, rows), BF16),
            vmem((2, 3, TILE, TILE), BF16),
            vmem((rows, width), F32),
            vmem((3, rows, width), BF16),
            vmem((2, 3, TILE, width), BF16),
            vmem((3, rows, width), BF16),
            vmem((2, 3, TILE, width), BF16),
            vmem((2, rows, 256), BF16),
            vmem((rows, 256), BF16),
            vmem((rows, width), BF16),
            vmem((2, 8, 16, width), F32),
            vmem((2, 8, 16, width), BF16),
            vmem((2, 7, 16, width), BF16),
            vmem((2, 8, 8, 128), F32),
            vmem((2, 7, 8, 128), F32),
            vmem((2, 8, 8, 128), F32),
            vmem((2, 8, 8, 128), F32),
            vmem((2, 8, 16, width), BF16),
            vmem((2, 8, 16, width), BF16),
            dma((4,)),
            dma((9,)),
            dma((9,)),
            dma((9,)),
            dma((9,)),
            dma((2,)),
            dma((70,)),
            dma((70,)),
            dma((16,)),
            dma((16,)),
            pltpu.SemaphoreType.REGULAR((4,)),
        ],
        compiler_params=pltpu.CompilerParams(collective_id=0, has_side_effects=True),
    )(
        block_list,
        block_count,
        features.reshape(rows, width),
        weight,
        edge_tiles.reshape(2, 9, TILE, TILE),
        grad_hidden.reshape(rows, width),
    )
    hidden, grad_features, grad_weight = pl.pallas_call(
        write_out,
        out_shape=[
            jax.ShapeDtypeStruct((rows, width), BF16),
            jax.ShapeDtypeStruct((rows, width), BF16),
            jax.ShapeDtypeStruct((2, 2, 8, 16, width), F32),
        ],
        in_specs=[local] * 3,
        out_specs=[anywhere] * 3,
        scratch_shapes=[dma((3,))],
    )(*[pltpu.with_memory_space_constraint(r, pltpu.VMEM) for r in results])
    grad_weight = grad_weight.reshape(width, width)
    return (hidden.reshape(features.shape), grad_features.reshape(features.shape), grad_weight)


def solution(mesh):
    placed = (
        P("loop", "section", None, None),
        P(),
        P("loop", "section", None, None, None),
        P("loop", "section", None),
        P("loop", "section"),
        P("loop", "section", None, None),
    )
    return jax.shard_map(
        per_device,
        mesh=mesh,
        in_specs=placed,
        out_specs=(P("loop", "section", None, None), P("loop", "section", None, None), P()),
        check_vma=False,
    )
```

```python
import functools
import math

import jax
import jax.numpy as jnp
from jax import lax
from jax.experimental import pallas as pl
from jax.experimental.pallas import tpu as pltpu
from jax.sharding import PartitionSpec as P

MESH = pl.DeviceIdType.MESH
F32 = jnp.float32
BF16 = jnp.bfloat16
TILE = 128
NX, NY, NZ, NYLO = 8, 8, 8, 4
LOOP, SECTION = 2 * NX * (NY // NYLO), NYLO * NZ


def dot(a, b):
    return jnp.dot(a, b, preferred_element_type=F32)


def dot_rows(a, b):
    return lax.dot_general(a, b, (((0,), (0,)), ((), ())), preferred_element_type=F32)


def dot_cols(a, b):
    return lax.dot_general(a, b, (((1,), (1,)), ((), ())), preferred_element_type=F32)


def kernel(
    scale,
    blist,
    bcount,
    feat,
    weight,
    edge,
    gh,
    hid_v,
    gf_v,
    gw_v,
    w_v,
    e_v,
    gh_v,
    a_mid,
    a_side,
    acc,
    pc,
    ps,
    pv,
    qc,
    qs,
    qv,
    ax,
    axp,
    back,
    part,
    s1,
    r1,
    s2,
    r2,
    r3,
    t2,
    t1,
    tp,
    in_sem,
    halo_ss,
    halo_rs,
    ghalo_ss,
    ghalo_rs,
    ax_sem,
    ar_ss,
    ar_rs,
    tp_ss,
    tp_rs,
    entered,
):
    L = lax.axis_index("loop")
    S = lax.axis_index("section")
    core = lax.rem(L, 2)
    x = lax.rem(L // 2, NX)
    y = (L // (2 * NX)) * NYLO + S // NZ
    z = lax.rem(S, NZ)

    def place(px, py, pz, pcore=core):
        return ((py // NYLO) * (2 * NX) + px * 2 + pcore, lax.rem(py, NYLO) * NZ + pz)

    def peer(axis, d):
        if axis == "x":
            k = lax.rem(x + d, NX)
            return k, place(k, y, z)
        if axis == "y":
            k = lax.rem(y + d, NY)
            return k, place(x, k, z)
        k = lax.rem(z + d, NZ)
        return k, place(x, y, k)

    out_row = L - 1 + 2 * core
    partner = (L + 1 - 2 * core, S)
    has_out = (out_row >= 0) & (out_row < LOOP)
    has_side = {-1: S > 0, 1: S < SECTION - 1}
    u_out, u_in = 2 * core, 2 * (1 - core)

    barrier = pltpu.get_barrier_semaphore()
    pl.semaphore_signal(barrier, inc=1, device_id=partner, device_id_type=MESH)

    rim = ((x == NX - 1) & (core == 1)) | ((x == 0) & (core == 0))
    border, direct = has_out & rim, has_out & jnp.logical_not(rim)
    way = lax.rem(y + 2 + 4 * core, NY) // (NY // 2)
    step = 2 - 4 * way

    def along(hops, across=False):
        py = lax.rem(y + hops + NY, NY)
        return place(NX - 1 - x, py, z, 1 - core) if across else place(x, py, z)

    @pl.when(direct)
    def _():
        pl.semaphore_signal(barrier, inc=1, device_id=(out_row, S), device_id_type=MESH)

    @pl.when(rim)
    def _():
        pl.semaphore_signal(barrier, inc=1, device_id=along(-step), device_id_type=MESH)
        pl.semaphore_signal(barrier, inc=1, device_id=along(step, True), device_id_type=MESH)

    @pl.when(border)
    def _():
        for hops in (-2, 2):
            for across in (False, True):
                pl.semaphore_signal(barrier, inc=1, device_id=along(hops, across), device_id_type=MESH)

    for dv in (-1, 1):

        @pl.when(has_side[dv])
        def _(dv=dv):
            pl.semaphore_signal(barrier, inc=1, device_id=(L, S + dv), device_id_type=MESH)

    def tell(sem, axes, hops):
        for axis in axes:
            for d in (hops, 8 - hops):
                pl.semaphore_signal(sem, inc=1, device_id=peer(axis, d)[1], device_id_type=MESH)

    tell(barrier, "xyz", 1)

    loads = [
        pltpu.make_async_copy(feat, pc.at[1], in_sem.at[0]),
        pltpu.make_async_copy(edge, e_v, in_sem.at[1]),
        pltpu.make_async_copy(weight, w_v, in_sem.at[2]),
        pltpu.make_async_copy(gh, gh_v, in_sem.at[3]),
    ]
    for load in loads:
        load.start()

    for mid, side in ((pc, ps), (qc, qs)):

        @pl.when(jnp.logical_not(has_out))
        def _(mid=mid, side=side):
            mid[u_out] = jnp.zeros((2 * TILE, 512), BF16)
            for k in range(2):
                side[k, u_out] = jnp.zeros((TILE, 512), BF16)

        for dv, k in ((-1, 0), (1, 1)):

            @pl.when(jnp.logical_not(has_side[dv]))
            def _(side=side, k=k):
                side[k] = jnp.zeros((3, TILE, 512), BF16)

    def halo(mid, side, via, ss, rs):
        def copy(n, src, dst, dev, m=None):
            return pltpu.make_async_remote_copy(
                src_ref=src,
                dst_ref=dst,
                send_sem=ss.at[n],
                recv_sem=rs.at[n if m is None else m],
                device_id=dev,
                device_id_type=MESH,
            )

        cut = {-1: pl.ds(0, TILE), 1: pl.ds(TILE, TILE)}
        slot = {-1: 1, 1: 0}
        jobs = {
            "partner": (copy(0, mid.at[1], mid.at[u_out], partner), None, None),
        }
        legs = []
        onward = copy(
            9,
            via,
            mid.at[u_in, pl.ds(pl.multiple_of(way * TILE, TILE), TILE)],
            along(step, True),
            1 + 7 * way,
        )
        for i, dv in enumerate((-1, 1)):
            dev = (L, S + dv)
            jobs["outer", dv] = (
                copy((1, 8)[i], mid.at[1, cut[dv]], mid.at[u_in, cut[dv]], (out_row, S)),
                direct,
                has_out,
            )
            legs.append(copy((1, 8)[i], mid.at[1, cut[dv]], via, along(-2 * dv), 9))
            jobs["side", dv] = (
                copy(2 + i, mid.at[1, cut[dv]], side.at[slot[dv], 1], dev),
                has_side[dv],
                has_side[-dv],
            )
            jobs["relay", dv] = (
                copy(4 + i, mid.at[u_out, cut[dv]], side.at[slot[dv], u_out], dev),
                has_side[dv] & has_out,
                has_side[-dv] & has_out,
            )
            jobs["share", dv] = (
                copy(6 + i, side.at[slot[dv], 1], side.at[slot[dv], u_out], partner),
                has_side[-dv],
                has_side[-dv],
            )

        def start(*keys):
            for key in keys:
                job, sends, _ = jobs[key]
                job.start() if sends is None else pl.when(sends)(job.start)

        def arrived(*keys):
            for key in keys:
                job, _, gets = jobs[key]
                job.wait_recv() if gets is None else pl.when(gets)(job.wait_recv)

        def start_border():
            @pl.when(border)
            def _():
                for leg in legs:
                    leg.start()

        def pass_on():
            @pl.when(rim)
            def _():
                legs[0].wait_recv()
                onward.start()

        def drained():
            for job, sends, _ in jobs.values():
                job.wait_send() if sends is None else pl.when(sends)(job.wait_send)

            @pl.when(border)
            def _():
                for leg in legs:
                    leg.wait_send()

            pl.when(rim)(onward.wait_send)

        return start, arrived, start_border, pass_on, drained

    p_start, p_arrived, p_border, p_pass_on, p_drained = halo(pc, ps, pv, halo_ss, halo_rs)
    q_start, q_arrived, q_border, q_pass_on, q_drained = halo(qc, qs, qv, ghalo_ss, ghalo_rs)
    sides = (("side", -1), ("side", 1))
    relays = (("relay", -1), ("relay", 1))
    shares = (("share", -1), ("share", 1))
    outers = (("outer", -1), ("outer", 1))

    loads[0].wait()
    greeted = direct.astype(jnp.int32) + 2 * rim.astype(jnp.int32) + 4 * border.astype(jnp.int32)
    greeted = greeted + sum(has_side[dv].astype(jnp.int32) for dv in (-1, 1))
    pl.semaphore_wait(barrier, 7 + greeted)
    p_border()
    p_start(*outers, *sides, "partner")
    tell(entered.at[0], "xy", 1)
    tell(entered.at[1], "z", 1)

    loads[1].wait()
    for b in range(2):
        bits = jnp.int32(0)
        for k in range(9):
            bits = bits | jnp.where(k < bcount[0, b], jnp.int32(1) << blist[0, b, k], 0)
        for s in range(9):
            tile = jnp.where(((bits >> s) & 1) == 1, e_v[b, s], jnp.zeros((TILE, TILE), BF16))
            u, v = s // 3, s % 3
            col = b + v
            if col in (1, 2):
                a_mid[u, b * TILE : (b + 1) * TILE, (col - 1) * TILE : col * TILE] = tile
            else:
                a_side[b, u] = tile

    def add_sides(side):
        for b in range(2):
            acc[b * TILE : (b + 1) * TILE] += sum(dot(a_side[b, u], side[b, u]) for u in range(3))

    acc[...] = dot(a_mid[1], pc[1])
    p_arrived("partner")
    acc[...] += dot(a_mid[u_in], pc[u_in])
    p_pass_on()
    for dv in (-1, 1):
        p_arrived(("side", dv))
        p_start(("share", dv))
    for dv in (-1, 1):
        p_arrived(("outer", dv))
        p_start(("relay", dv))
    pl.semaphore_wait(entered.at[0], 4)
    tell(entered.at[2], "xy", 2)
    pl.semaphore_wait(entered.at[1], 2)
    tell(entered.at[3], "z", 2)
    acc[...] += dot(a_mid[u_out], pc[u_out])
    p_arrived(*shares, *relays)
    add_sides(ps)

    for half in range(2):
        ax[half] = acc[:, half * 256 : (half + 1) * 256].astype(BF16)
    ax_copy = pltpu.make_async_remote_copy(
        src_ref=ax.at[1 - core],
        dst_ref=axp,
        send_sem=ax_sem.at[0],
        recv_sem=ax_sem.at[1],
        device_id=partner,
        device_id_type=MESH,
    )
    ax_copy.start()
    loads[2].wait()
    acc[...] = dot(ax[0], w_v[:256]) + dot(ax[1], w_v[256:])
    loads[3].wait()
    for r in range(0, 256, 32):
        p = acc[r : r + 32]
        sig = jax.nn.sigmoid(p)
        hid_v[r : r + 32] = (p * sig).astype(BF16)
        g = gh_v[r : r + 32].astype(F32)
        qc[1, r : r + 32] = (g * sig * (1.0 + p * (1.0 - sig))).astype(BF16)

    q_start("partner")

    own_part = dot_rows(ax[core], qc[1])
    part[...] = own_part.reshape(2, 8, 16, 512)
    ax_copy.wait()

    q_arrived("partner")
    part[...] += dot_rows(axp[...], qc[u_in]).reshape(2, 8, 16, 512)
    s1[...] = part[...].astype(BF16)

    first = ("y", "x")
    second = ("x", "y")
    at = {"x": x, "y": y, "z": z}

    def ar(stage, h, d, src, dst, dev):
        k = (stage * 2 + h) * 7 + d - 1
        return pltpu.make_async_remote_copy(
            src_ref=src,
            dst_ref=dst,
            send_sem=ar_ss.at[k],
            recv_sem=ar_rs.at[k],
            device_id=dev,
            device_id_type=MESH,
        )

    sent = []
    both = [(h, d) for d in (4, 3, 5, 2, 6, 1, 7) for h in range(2)]

    def run(stage, make):
        copies = []
        for h, d in both:
            c = make(stage, h, d)
            c.start()
            copies.append(c)
        sent.extend(copies)
        return copies

    def make1(stage, h, d):
        k, dev = peer(first[h], d)
        return ar(stage, h, d, s1.at[h, k], r1.at[h, d - 1], dev)

    pl.semaphore_wait(entered.at[2], 4)
    copies = run(0, make1)
    q_border()
    q_start(*outers, *sides)
    for c in copies:
        c.wait_recv()
    for h in range(2):
        total = part[h, at[first[h]]]
        for d in range(7):
            total = total + r1[h, d].astype(F32)
        for t in range(8):
            s2[h, t] = total[(t // 4) * 8 : (t // 4) * 8 + 8, (t % 4) * 128 : (t % 4) * 128 + 128]

    def make2(stage, h, d):
        k, dev = peer(second[h], d)
        return ar(stage, h, d, s2.at[h, k], r2.at[h, d - 1], dev)

    copies = run(1, make2)
    q_pass_on()
    for c in copies:
        c.wait_recv()
    for h in range(2):
        total = s2[h, at[second[h]]]
        for d in range(7):
            total = total + r2[h, d]
        r3[h, z] = total

    def make3(stage, h, d):
        _, dev = peer("z", d)
        return ar(stage, h, d, r3.at[h, z], r3.at[h, z], dev)

    pl.semaphore_wait(entered.at[3], 2)
    copies = run(2, make3)
    for dv in (-1, 1):
        q_arrived(("side", dv))
        q_start(("share", dv))
    for c in copies:
        c.wait_recv()
    for h in range(2):
        total = r3[h, 0]
        for d in range(1, 8):
            total = total + r3[h, d]
        t2[h, at[second[h]]] = total

    def make4(stage, h, d):
        _, dev = peer(second[h], d)
        return ar(stage, h, d, t2.at[h, at[second[h]]], t2.at[h, at[second[h]]], dev)

    copies = run(3, make4)
    for dv in (-1, 1):
        q_arrived(("outer", dv))
        q_start(("relay", dv))
    acc[...] = dot(a_mid[0], qc[0]) + dot(a_mid[1], qc[1]) + dot(a_mid[2], qc[2])
    for c in copies:
        c.wait_recv()
    for h in range(2):
        lines = [jnp.concatenate([t2[h, 4 * r + k] for k in range(4)], axis=1) for r in range(2)]
        t1[h, at[first[h]]] = jnp.concatenate(lines, axis=0).astype(BF16)

    def make5(stage, h, d):
        _, dev = peer(first[h], d)
        return ar(stage, h, d, t1.at[h, at[first[h]]], t1.at[h, at[first[h]]], dev)

    copies = run(4, make5)

    def pair(h, d):
        k = lax.rem(at[first[h]] + (8 - d), 8)
        c = pltpu.make_async_remote_copy(
            src_ref=t1.at[h, k],
            dst_ref=tp.at[h, k],
            send_sem=tp_ss.at[h * 8 + d],
            recv_sem=tp_rs.at[h * 8 + d],
            device_id=partner,
            device_id_type=MESH,
        )
        c.start()
        return c

    pairs = [pair(h, 0) for h in range(2)]

    q_arrived(*shares, *relays)
    add_sides(qs)
    back[...] = acc[...].astype(BF16)
    gf_v[...] = dot_cols(back[...], w_v[...]).astype(BF16)

    for (h, d), c in sorted(zip(both, copies), key=lambda e: (min(e[0][1], 8 - e[0][1]), e[0])):
        c.wait_recv()
        pairs.append(pair(h, d))
    gw_v[core] = t1[...].astype(F32) * scale
    for c in pairs:
        c.wait_recv()
    gw_v[1 - core] = tp[...].astype(F32) * scale

    for c in sent + pairs:
        c.wait_send()
    p_drained()
    q_drained()


def write_out(hid_v, gf_v, gw_v, hid_o, gf_o, gw_o, sem):
    copies = [
        pltpu.make_async_copy(gw_v, gw_o, sem.at[0]),
        pltpu.make_async_copy(hid_v, hid_o, sem.at[1]),
        pltpu.make_async_copy(gf_v, gf_o, sem.at[2]),
    ]
    for copy in copies:
        copy.start()
    for copy in copies:
        copy.wait()


def per_device(features, weight, edge_tiles, block_list, block_count, grad_hidden):
    rows, width = 2 * TILE, features.shape[3]
    nodes = LOOP * SECTION * rows
    local = pl.BlockSpec(memory_space=pltpu.VMEM)
    anywhere = pl.BlockSpec(memory_space=pl.ANY)
    scalars = pl.BlockSpec(memory_space=pltpu.SMEM)
    dma = pltpu.SemaphoreType.DMA
    vmem = pltpu.VMEM
    results = pl.pallas_call(
        functools.partial(kernel, 1.0 / math.sqrt(nodes)),
        out_shape=[
            pltpu.VMEM((rows, width), BF16),
            pltpu.VMEM((rows, width), BF16),
            pltpu.VMEM((2, 2, 8, 16, width), F32),
        ],
        in_specs=[scalars, scalars, anywhere, anywhere, anywhere, anywhere],
        out_specs=[local] * 3,
        scratch_shapes=[
            vmem((width, width), BF16),
            vmem((2, 9, TILE, TILE), BF16),
            vmem((rows, width), BF16),
            vmem((3, rows, rows), BF16),
            vmem((2, 3, TILE, TILE), BF16),
            vmem((rows, width), F32),
            vmem((3, rows, width), BF16),
            vmem((2, 3, TILE, width), BF16),
            vmem((TILE, width), BF16),
            vmem((3, rows, width), BF16),
            vmem((2, 3, TILE, width), BF16),
            vmem((TILE, width), BF16),
            vmem((2, rows, 256), BF16),
            vmem((rows, 256), BF16),
            vmem((rows, width), BF16),
            vmem((2, 8, 16, width), F32),
            vmem((2, 8, 16, width), BF16),
            vmem((2, 7, 16, width), BF16),
            vmem((2, 8, 8, 128), F32),
            vmem((2, 7, 8, 128), F32),
            vmem((2, 8, 8, 128), F32),
            vmem((2, 8, 8, 128), F32),
            vmem((2, 8, 16, width), BF16),
            vmem((2, 8, 16, width), BF16),
            dma((4,)),
            dma((10,)),
            dma((10,)),
            dma((10,)),
            dma((10,)),
            dma((2,)),
            dma((70,)),
            dma((70,)),
            dma((16,)),
            dma((16,)),
            pltpu.SemaphoreType.REGULAR((4,)),
        ],
        compiler_params=pltpu.CompilerParams(collective_id=0, has_side_effects=True),
    )(
        block_list,
        block_count,
        features.reshape(rows, width),
        weight,
        edge_tiles.reshape(2, 9, TILE, TILE),
        grad_hidden.reshape(rows, width),
    )
    hidden, grad_features, grad_weight = pl.pallas_call(
        write_out,
        out_shape=[
            jax.ShapeDtypeStruct((rows, width), BF16),
            jax.ShapeDtypeStruct((rows, width), BF16),
            jax.ShapeDtypeStruct((2, 2, 8, 16, width), F32),
        ],
        in_specs=[local] * 3,
        out_specs=[anywhere] * 3,
        scratch_shapes=[dma((3,))],
    )(*[pltpu.with_memory_space_constraint(r, pltpu.VMEM) for r in results])
    grad_weight = grad_weight.reshape(width, width)
    return (hidden.reshape(features.shape), grad_features.reshape(features.shape), grad_weight)


def solution(mesh):
    placed = (
        P("loop", "section", None, None),
        P(),
        P("loop", "section", None, None, None),
        P("loop", "section", None),
        P("loop", "section"),
        P("loop", "section", None, None),
    )
    return jax.shard_map(
        per_device,
        mesh=mesh,
        in_specs=placed,
        out_specs=(P("loop", "section", None, None), P("loop", "section", None, None), P()),
        check_vma=False,
    )
```

```python
import functools
import math

import jax
import jax.numpy as jnp
from jax import lax
from jax.experimental import pallas as pl
from jax.experimental.pallas import tpu as pltpu
from jax.sharding import PartitionSpec as P

MESH = pl.DeviceIdType.MESH
F32 = jnp.float32
BF16 = jnp.bfloat16
TILE = 128
NX, NY, NZ, NYLO = 8, 8, 8, 4
LOOP, SECTION = 2 * NX * (NY // NYLO), NYLO * NZ


def dot(a, b):
    return jnp.dot(a, b, preferred_element_type=F32)


def dot_rows(a, b):
    return lax.dot_general(a, b, (((0,), (0,)), ((), ())), preferred_element_type=F32)


def dot_cols(a, b):
    return lax.dot_general(a, b, (((1,), (1,)), ((), ())), preferred_element_type=F32)


def kernel(
    scale,
    blist_h,
    bcount_h,
    feat,
    weight,
    edge,
    gh,
    hid_v,
    gf_v,
    gw_v,
    w_v,
    e_v,
    gh_v,
    a_mid,
    a_side,
    acc,
    pc,
    ps,
    pv,
    qc,
    qs,
    qv,
    ax,
    axp,
    back,
    part,
    s1,
    r1,
    rx,
    t1,
    tp,
    blist,
    bcount,
    in_sem,
    halo_ss,
    halo_rs,
    ghalo_ss,
    ghalo_rs,
    ax_sem,
    ar_ss,
    ar_rs,
    tp_ss,
    tp_rs,
    entered,
):
    L = lax.axis_index("loop")
    S = lax.axis_index("section")
    core = lax.rem(L, 2)
    x = lax.rem(L // 2, NX)
    y = (L // (2 * NX)) * NYLO + S // NZ
    z = lax.rem(S, NZ)

    def place(px, py, pz, pcore=core):
        return ((py // NYLO) * (2 * NX) + px * 2 + pcore, lax.rem(py, NYLO) * NZ + pz)

    def peer(axis, d):
        if axis == "x":
            k = lax.rem(x + d, NX)
            return k, place(k, y, z)
        if axis == "y":
            k = lax.rem(y + d, NY)
            return k, place(x, k, z)
        k = lax.rem(z + d, NZ)
        return k, place(x, y, k)

    out_row = L - 1 + 2 * core
    partner = (L + 1 - 2 * core, S)
    has_out = (out_row >= 0) & (out_row < LOOP)
    has_side = {-1: S > 0, 1: S < SECTION - 1}
    u_out, u_in = 2 * core, 2 * (1 - core)

    barrier = pltpu.get_barrier_semaphore()
    pl.semaphore_signal(barrier, inc=1, device_id=partner, device_id_type=MESH)

    rim = ((x == NX - 1) & (core == 1)) | ((x == 0) & (core == 0))
    border, direct = has_out & rim, has_out & jnp.logical_not(rim)
    way = lax.rem(y + 2 + 4 * core, NY) // (NY // 2)
    step = 2 - 4 * way

    def along(hops, across=False):
        py = lax.rem(y + hops + NY, NY)
        return place(NX - 1 - x, py, z, 1 - core) if across else place(x, py, z)

    @pl.when(direct)
    def _():
        pl.semaphore_signal(barrier, inc=1, device_id=(out_row, S), device_id_type=MESH)

    @pl.when(rim)
    def _():
        pl.semaphore_signal(barrier, inc=1, device_id=along(-step), device_id_type=MESH)
        pl.semaphore_signal(barrier, inc=1, device_id=along(step, True), device_id_type=MESH)

    @pl.when(border)
    def _():
        for hops in (-2, 2):
            for across in (False, True):
                pl.semaphore_signal(barrier, inc=1, device_id=along(hops, across), device_id_type=MESH)

    for dv in (-1, 1):

        @pl.when(has_side[dv])
        def _(dv=dv):
            pl.semaphore_signal(barrier, inc=1, device_id=(L, S + dv), device_id_type=MESH)

    def tell(sem, axes, hops):
        for axis in axes:
            for d in (hops, 8 - hops):
                pl.semaphore_signal(sem, inc=1, device_id=peer(axis, d)[1], device_id_type=MESH)

    tell(barrier, "xyz", 1)

    loads = [
        pltpu.make_async_copy(feat, pc.at[1], in_sem.at[0]),
        pltpu.make_async_copy(edge, e_v, in_sem.at[1]),
        pltpu.make_async_copy(weight, w_v, in_sem.at[2]),
        pltpu.make_async_copy(gh, gh_v, in_sem.at[3]),
        pltpu.make_async_copy(blist_h, blist, in_sem.at[4]),
        pltpu.make_async_copy(bcount_h, bcount, in_sem.at[5]),
    ]
    for load in loads:
        load.start()

    for mid, side in ((pc, ps), (qc, qs)):

        @pl.when(jnp.logical_not(has_out))
        def _(mid=mid, side=side):
            mid[u_out] = jnp.zeros((2 * TILE, 512), BF16)
            for k in range(2):
                side[k, u_out] = jnp.zeros((TILE, 512), BF16)

        for dv, k in ((-1, 0), (1, 1)):

            @pl.when(jnp.logical_not(has_side[dv]))
            def _(side=side, k=k):
                side[k] = jnp.zeros((3, TILE, 512), BF16)

    def halo(mid, side, via, ss, rs):
        def copy(n, src, dst, dev, m=None):
            return pltpu.make_async_remote_copy(
                src_ref=src,
                dst_ref=dst,
                send_sem=ss.at[n],
                recv_sem=rs.at[n if m is None else m],
                device_id=dev,
                device_id_type=MESH,
            )

        cut = {-1: pl.ds(0, TILE), 1: pl.ds(TILE, TILE)}
        slot = {-1: 1, 1: 0}
        jobs = {
            "partner": (copy(0, mid.at[1], mid.at[u_out], partner), None, None),
        }
        legs = []
        onward = copy(
            9,
            via,
            mid.at[u_in, pl.ds(pl.multiple_of(way * TILE, TILE), TILE)],
            along(step, True),
            1 + 7 * way,
        )
        for i, dv in enumerate((-1, 1)):
            dev = (L, S + dv)
            jobs["outer", dv] = (
                copy((1, 8)[i], mid.at[1, cut[dv]], mid.at[u_in, cut[dv]], (out_row, S)),
                direct,
                has_out,
            )
            legs.append(copy((1, 8)[i], mid.at[1, cut[dv]], via, along(-2 * dv), 9))
            jobs["side", dv] = (
                copy(2 + i, mid.at[1, cut[dv]], side.at[slot[dv], 1], dev),
                has_side[dv],
                has_side[-dv],
            )
            jobs["relay", dv] = (
                copy(4 + i, mid.at[u_out, cut[dv]], side.at[slot[dv], u_out], dev),
                has_side[dv] & has_out,
                has_side[-dv] & has_out,
            )
            jobs["share", dv] = (
                copy(6 + i, side.at[slot[dv], 1], side.at[slot[dv], u_out], partner),
                has_side[-dv],
                has_side[-dv],
            )

        def start(*keys):
            for key in keys:
                job, sends, _ = jobs[key]
                job.start() if sends is None else pl.when(sends)(job.start)

        def arrived(*keys):
            for key in keys:
                job, _, gets = jobs[key]
                job.wait_recv() if gets is None else pl.when(gets)(job.wait_recv)

        def start_border():
            @pl.when(border)
            def _():
                for leg in legs:
                    leg.start()

        def pass_on():
            @pl.when(rim)
            def _():
                legs[0].wait_recv()
                onward.start()

        def drained():
            for job, sends, _ in jobs.values():
                job.wait_send() if sends is None else pl.when(sends)(job.wait_send)

            @pl.when(border)
            def _():
                for leg in legs:
                    leg.wait_send()

            pl.when(rim)(onward.wait_send)

        return start, arrived, start_border, pass_on, drained

    p_start, p_arrived, p_border, p_pass_on, p_drained = halo(pc, ps, pv, halo_ss, halo_rs)
    q_start, q_arrived, q_border, q_pass_on, q_drained = halo(qc, qs, qv, ghalo_ss, ghalo_rs)
    sides = (("side", -1), ("side", 1))
    relays = (("relay", -1), ("relay", 1))
    shares = (("share", -1), ("share", 1))
    outers = (("outer", -1), ("outer", 1))

    loads[0].wait()
    greeted = direct.astype(jnp.int32) + 2 * rim.astype(jnp.int32) + 4 * border.astype(jnp.int32)
    greeted = greeted + sum(has_side[dv].astype(jnp.int32) for dv in (-1, 1))
    pl.semaphore_wait(barrier, 7 + greeted)
    p_border()
    p_start(*outers, *sides, "partner")
    tell(entered.at[0], "xy", 1)
    tell(entered.at[1], "z", 1)

    for k in (1, 4, 5):
        loads[k].wait()
    for b in range(2):
        bits = jnp.int32(0)
        for k in range(9):
            bits = bits | jnp.where(k < bcount[0, b], jnp.int32(1) << blist[0, b, k], 0)
        for s in range(9):
            tile = jnp.where(((bits >> s) & 1) == 1, e_v[b, s], jnp.zeros((TILE, TILE), BF16))
            u, v = s // 3, s % 3
            col = b + v
            if col in (1, 2):
                a_mid[u, b * TILE : (b + 1) * TILE, (col - 1) * TILE : col * TILE] = tile
            else:
                a_side[b, u] = tile

    def add_sides(side):
        for b in range(2):
            acc[b * TILE : (b + 1) * TILE] += sum(dot(a_side[b, u], side[b, u]) for u in range(3))

    acc[...] = dot(a_mid[1], pc[1])
    p_arrived("partner")
    acc[...] += dot(a_mid[u_in], pc[u_in])
    p_pass_on()

    def corners():
        for dv in (-1, 1):
            p_arrived(("outer", dv))
            p_start(("relay", dv))

    pl.when(direct)(corners)
    for dv in (-1, 1):
        p_arrived(("side", dv))
        p_start(("share", dv))
    pl.when(border)(corners)
    pl.semaphore_wait(entered.at[0], 4)
    tell(entered.at[2], "xy", 2)
    pl.semaphore_wait(entered.at[1], 2)
    tell(entered.at[3], "z", 2)
    acc[...] += dot(a_mid[u_out], pc[u_out])
    p_arrived(*shares, *relays)
    add_sides(ps)

    for half in range(2):
        ax[half] = acc[:, half * 256 : (half + 1) * 256].astype(BF16)
    ax_copy = pltpu.make_async_remote_copy(
        src_ref=ax.at[1 - core],
        dst_ref=axp,
        send_sem=ax_sem.at[0],
        recv_sem=ax_sem.at[1],
        device_id=partner,
        device_id_type=MESH,
    )
    ax_copy.start()
    loads[2].wait()
    acc[...] = dot(ax[0], w_v[:256]) + dot(ax[1], w_v[256:])
    loads[3].wait()
    for r in range(0, 256, 32):
        p = acc[r : r + 32]
        sig = jax.nn.sigmoid(p)
        hid_v[r : r + 32] = (p * sig).astype(BF16)
        g = gh_v[r : r + 32].astype(F32)
        qc[1, r : r + 32] = (g * sig * (1.0 + p * (1.0 - sig))).astype(BF16)

    q_start("partner")

    own_part = dot_rows(ax[core], qc[1])
    part[...] = own_part.reshape(2, 8, 16, 512)
    ax_copy.wait()

    q_arrived("partner")
    part[...] += dot_rows(axp[...], qc[u_in]).reshape(2, 8, 16, 512)
    s1[...] = part[...].astype(BF16)

    first = ("y", "x")
    second = ("x", "y")
    at = {"x": x, "y": y, "z": z}

    def ar(k, src, dst, dev):
        return pltpu.make_async_remote_copy(
            src_ref=src,
            dst_ref=dst,
            send_sem=ar_ss.at[k],
            recv_sem=ar_rs.at[k],
            device_id=dev,
            device_id_type=MESH,
        )

    sent = []
    far_first = (4, 3, 5, 2, 6, 1, 7)
    both = [(h, d) for d in far_first for h in range(2)]
    quarters = [(h, c) for h in range(2) for c in range(2)]

    def run(copies):
        for c in copies:
            c.start()
        sent.extend(copies)
        return copies

    def scatter(h, d):
        k, dev = peer(first[h], d)
        return ar(h * 7 + d - 1, s1.at[h, k], r1.at[h, d - 1], dev)

    def axis_of(stage, h, c):
        return "z" if stage == c else second[h]

    def exchange(stage, h, c, d):
        _, dev = peer(axis_of(stage, h, c), d)
        slot = rx.at[stage, h, c, at[axis_of(stage, h, c)]]
        return ar(14 + ((stage * 2 + h) * 2 + c) * 7 + d - 1, slot, slot, dev)

    def exchange_all(stage):
        return run([exchange(stage, h, c, d) for d in far_first for h, c in quarters])

    def summed(stage, h, c):
        total = rx[stage, h, c, 0].astype(F32)
        for k in range(1, 8):
            total = total + rx[stage, h, c, k].astype(F32)
        return total.astype(BF16)

    def gather(h, d):
        _, dev = peer(first[h], d)
        slot = t1.at[h, at[first[h]]]
        return ar(70 + h * 7 + d - 1, slot, slot, dev)

    pl.semaphore_wait(entered.at[2], 4)
    copies = run([scatter(h, d) for h, d in both])
    q_border()
    q_start(*outers, *sides)
    for c in copies:
        c.wait_recv()
    for h in range(2):
        total = part[h, at[first[h]]]
        for d in range(7):
            total = total + r1[h, d].astype(F32)
        for c in range(2):
            rx[1, h, c, at[axis_of(1, h, c)]] = total[:, c * 256 : (c + 1) * 256].astype(BF16)

    pl.semaphore_wait(entered.at[3], 2)
    copies = exchange_all(1)
    q_pass_on()
    for dv in (-1, 1):
        q_arrived(("side", dv))
        q_start(("share", dv))
    for c in copies:
        c.wait_recv()
    for h, c in quarters:
        rx[0, h, c, at[axis_of(0, h, c)]] = summed(1, h, c)
    copies = exchange_all(0)

    def q_corners():
        for dv in (-1, 1):
            q_arrived(("outer", dv))
            q_start(("relay", dv))

    pl.when(direct)(q_corners)
    for c in copies:
        c.wait_recv()
    for h, c in quarters:
        t1[h, at[first[h]], :, c * 256 : (c + 1) * 256] = summed(0, h, c)
    copies = run([gather(h, d) for h, d in both])

    def pair(h, d):
        k = lax.rem(at[first[h]] + (8 - d), 8)
        c = pltpu.make_async_remote_copy(
            src_ref=t1.at[h, k],
            dst_ref=tp.at[h, k],
            send_sem=tp_ss.at[h * 8 + d],
            recv_sem=tp_rs.at[h * 8 + d],
            device_id=partner,
            device_id_type=MESH,
        )
        c.start()
        return c

    pairs = [pair(h, 0) for h in range(2)]
    pl.when(border)(q_corners)
    acc[...] = dot(a_mid[0], qc[0]) + dot(a_mid[1], qc[1]) + dot(a_mid[2], qc[2])

    for (h, d), c in sorted(zip(both, copies), key=lambda e: (min(e[0][1], 8 - e[0][1]), e[0])):
        c.wait_recv()
        pairs.append(pair(h, d))
    q_arrived(*shares, *relays)
    add_sides(qs)
    back[...] = acc[...].astype(BF16)
    gf_v[...] = dot_cols(back[...], w_v[...]).astype(BF16)

    gw_v[core] = t1[...].astype(F32) * scale
    for c in pairs:
        c.wait_recv()
    gw_v[1 - core] = tp[...].astype(F32) * scale

    for c in sent + pairs:
        c.wait_send()
    p_drained()
    q_drained()


def write_out(hid_v, gf_v, gw_v, hid_o, gf_o, gw_o, sem):
    copies = [
        pltpu.make_async_copy(gw_v, gw_o, sem.at[0]),
        pltpu.make_async_copy(hid_v, hid_o, sem.at[1]),
        pltpu.make_async_copy(gf_v, gf_o, sem.at[2]),
    ]
    for copy in copies:
        copy.start()
    for copy in copies:
        copy.wait()


def per_device(features, weight, edge_tiles, block_list, block_count, grad_hidden):
    rows, width = 2 * TILE, features.shape[3]
    nodes = LOOP * SECTION * rows
    local = pl.BlockSpec(memory_space=pltpu.VMEM)
    anywhere = pl.BlockSpec(memory_space=pl.ANY)
    dma = pltpu.SemaphoreType.DMA
    vmem = pltpu.VMEM
    results = pl.pallas_call(
        functools.partial(kernel, 1.0 / math.sqrt(nodes)),
        out_shape=[
            pltpu.VMEM((rows, width), BF16),
            pltpu.VMEM((rows, width), BF16),
            pltpu.VMEM((2, 2, 8, 16, width), F32),
        ],
        in_specs=[anywhere] * 6,
        out_specs=[local] * 3,
        scratch_shapes=[
            vmem((width, width), BF16),
            vmem((2, 9, TILE, TILE), BF16),
            vmem((rows, width), BF16),
            vmem((3, rows, rows), BF16),
            vmem((2, 3, TILE, TILE), BF16),
            vmem((rows, width), F32),
            vmem((3, rows, width), BF16),
            vmem((2, 3, TILE, width), BF16),
            vmem((TILE, width), BF16),
            vmem((3, rows, width), BF16),
            vmem((2, 3, TILE, width), BF16),
            vmem((TILE, width), BF16),
            vmem((2, rows, 256), BF16),
            vmem((rows, 256), BF16),
            vmem((rows, width), BF16),
            vmem((2, 8, 16, width), F32),
            vmem((2, 8, 16, width), BF16),
            vmem((2, 7, 16, width), BF16),
            vmem((2, 2, 2, 8, 16, 256), BF16),
            vmem((2, 8, 16, width), BF16),
            vmem((2, 8, 16, width), BF16),
            pltpu.SMEM((1, 2, 9), jnp.int32),
            pltpu.SMEM((1, 2), jnp.int32),
            dma((6,)),
            dma((10,)),
            dma((10,)),
            dma((10,)),
            dma((10,)),
            dma((2,)),
            dma((84,)),
            dma((84,)),
            dma((16,)),
            dma((16,)),
            pltpu.SemaphoreType.REGULAR((4,)),
        ],
        compiler_params=pltpu.CompilerParams(collective_id=0, has_side_effects=True),
    )(
        block_list,
        block_count,
        features.reshape(rows, width),
        weight,
        edge_tiles.reshape(2, 9, TILE, TILE),
        grad_hidden.reshape(rows, width),
    )
    hidden, grad_features, grad_weight = pl.pallas_call(
        write_out,
        out_shape=[
            jax.ShapeDtypeStruct((rows, width), BF16),
            jax.ShapeDtypeStruct((rows, width), BF16),
            jax.ShapeDtypeStruct((2, 2, 8, 16, width), F32),
        ],
        in_specs=[local] * 3,
        out_specs=[anywhere] * 3,
        scratch_shapes=[dma((3,))],
    )(*[pltpu.with_memory_space_constraint(r, pltpu.VMEM) for r in results])
    grad_weight = grad_weight.reshape(width, width)
    return (hidden.reshape(features.shape), grad_features.reshape(features.shape), grad_weight)


def solution(mesh):
    placed = (
        P("loop", "section", None, None),
        P(),
        P("loop", "section", None, None, None),
        P("loop", "section", None),
        P("loop", "section"),
        P("loop", "section", None, None),
    )
    return jax.shard_map(
        per_device,
        mesh=mesh,
        in_specs=placed,
        out_specs=(P("loop", "section", None, None), P("loop", "section", None, None), P()),
        check_vma=False,
    )
```

```python
import functools
import math

import jax
import jax.numpy as jnp
from jax import lax
from jax.experimental import pallas as pl
from jax.experimental.pallas import tpu as pltpu
from jax.sharding import PartitionSpec as P

MESH = pl.DeviceIdType.MESH
F32 = jnp.float32
BF16 = jnp.bfloat16
TILE = 128
NX, NY, NZ, NYLO = 8, 8, 8, 4
LOOP, SECTION = 2 * NX * (NY // NYLO), NYLO * NZ


def dot(a, b):
    return jnp.dot(a, b, preferred_element_type=F32)


def dot_rows(a, b):
    return lax.dot_general(a, b, (((0,), (0,)), ((), ())), preferred_element_type=F32)


def dot_cols(a, b):
    return lax.dot_general(a, b, (((1,), (1,)), ((), ())), preferred_element_type=F32)


def kernel(
    scale,
    blist_h,
    bcount_h,
    feat,
    weight,
    edge,
    gh,
    hid_v,
    gf_v,
    gw_v,
    w_v,
    e_v,
    gh_v,
    a_mid,
    a_side,
    acc,
    pc,
    ps,
    qc,
    qs,
    ax,
    axp,
    back,
    part,
    s1,
    r1,
    rx,
    t1,
    tp,
    blist,
    bcount,
    in_sem,
    halo_ss,
    halo_rs,
    ghalo_ss,
    ghalo_rs,
    ax_sem,
    ar_ss,
    ar_rs,
    tp_ss,
    tp_rs,
    entered,
):
    L = lax.axis_index("loop")
    S = lax.axis_index("section")
    core = lax.rem(L, 2)
    x = lax.rem(L // 2, NX)
    y = (L // (2 * NX)) * NYLO + S // NZ
    z = lax.rem(S, NZ)

    def place(px, py, pz):
        return ((py // NYLO) * (2 * NX) + px * 2 + core, lax.rem(py, NYLO) * NZ + pz)

    def peer(axis, d):
        if axis == "x":
            k = lax.rem(x + d, NX)
            return k, place(k, y, z)
        if axis == "y":
            k = lax.rem(y + d, NY)
            return k, place(x, k, z)
        k = lax.rem(z + d, NZ)
        return k, place(x, y, k)

    out_row = L - 1 + 2 * core
    partner = (L + 1 - 2 * core, S)
    has_out = (out_row >= 0) & (out_row < LOOP)
    has_side = {-1: S > 0, 1: S < SECTION - 1}
    u_out, u_in = 2 * core, 2 * (1 - core)

    barrier = pltpu.get_barrier_semaphore()
    pl.semaphore_signal(barrier, inc=1, device_id=partner, device_id_type=MESH)

    @pl.when(has_out)
    def _():
        pl.semaphore_signal(barrier, inc=1, device_id=(out_row, S), device_id_type=MESH)

    for dv in (-1, 1):

        @pl.when(has_side[dv])
        def _(dv=dv):
            pl.semaphore_signal(barrier, inc=1, device_id=(L, S + dv), device_id_type=MESH)

    def tell(sem, axes, hops):
        for axis in axes:
            for d in (hops, 8 - hops):
                pl.semaphore_signal(sem, inc=1, device_id=peer(axis, d)[1], device_id_type=MESH)

    tell(barrier, "xyz", 1)

    loads = [
        pltpu.make_async_copy(feat, pc.at[1], in_sem.at[0]),
        pltpu.make_async_copy(edge, e_v, in_sem.at[1]),
        pltpu.make_async_copy(weight, w_v, in_sem.at[2]),
        pltpu.make_async_copy(gh, gh_v, in_sem.at[3]),
        pltpu.make_async_copy(blist_h, blist, in_sem.at[4]),
        pltpu.make_async_copy(bcount_h, bcount, in_sem.at[5]),
    ]
    for load in loads:
        load.start()

    for mid, side in ((pc, ps), (qc, qs)):

        @pl.when(jnp.logical_not(has_out))
        def _(mid=mid, side=side):
            mid[u_out] = jnp.zeros((2 * TILE, 512), BF16)
            for k in range(2):
                side[k, u_out] = jnp.zeros((TILE, 512), BF16)

        for dv, k in ((-1, 0), (1, 1)):

            @pl.when(jnp.logical_not(has_side[dv]))
            def _(side=side, k=k):
                side[k] = jnp.zeros((3, TILE, 512), BF16)

    def halo(mid, side, ss, rs):
        def copy(n, src, dst, dev):
            return pltpu.make_async_remote_copy(
                src_ref=src,
                dst_ref=dst,
                send_sem=ss.at[n],
                recv_sem=rs.at[n],
                device_id=dev,
                device_id_type=MESH,
            )

        cut = {-1: pl.ds(0, TILE), 1: pl.ds(TILE, TILE)}
        slot = {-1: 1, 1: 0}
        jobs = {
            "partner": (copy(0, mid.at[1], mid.at[u_out], partner), None, None),
        }
        for i, dv in enumerate((-1, 1)):
            dev = (L, S + dv)
            jobs["outer", dv] = (
                copy((1, 8)[i], mid.at[1, cut[dv]], mid.at[u_in, cut[dv]], (out_row, S)),
                has_out,
                has_out,
            )
            jobs["side", dv] = (
                copy(2 + i, mid.at[1, cut[dv]], side.at[slot[dv], 1], dev),
                has_side[dv],
                has_side[-dv],
            )
            jobs["relay", dv] = (
                copy(4 + i, mid.at[u_out, cut[dv]], side.at[slot[dv], u_out], dev),
                has_side[dv] & has_out,
                has_side[-dv] & has_out,
            )
            jobs["share", dv] = (
                copy(6 + i, side.at[slot[dv], 1], side.at[slot[dv], u_out], partner),
                has_side[-dv],
                has_side[-dv],
            )

        def start(*keys):
            for key in keys:
                job, sends, _ = jobs[key]
                job.start() if sends is None else pl.when(sends)(job.start)

        def arrived(*keys):
            for key in keys:
                job, _, gets = jobs[key]
                job.wait_recv() if gets is None else pl.when(gets)(job.wait_recv)

        def drained():
            for job, sends, _ in jobs.values():
                job.wait_send() if sends is None else pl.when(sends)(job.wait_send)

        return start, arrived, drained

    p_start, p_arrived, p_drained = halo(pc, ps, halo_ss, halo_rs)
    q_start, q_arrived, q_drained = halo(qc, qs, ghalo_ss, ghalo_rs)
    sides = (("side", -1), ("side", 1))
    relays = (("relay", -1), ("relay", 1))
    shares = (("share", -1), ("share", 1))
    outers = (("outer", -1), ("outer", 1))

    loads[0].wait()
    greeted = has_out.astype(jnp.int32) + sum(has_side[dv].astype(jnp.int32) for dv in (-1, 1))
    pl.semaphore_wait(barrier, 7 + greeted)
    p_start(*outers, *sides, "partner")
    tell(entered.at[0], "xy", 1)
    tell(entered.at[1], "z", 1)

    for k in (1, 4, 5):
        loads[k].wait()
    for b in range(2):
        bits = jnp.int32(0)
        for k in range(9):
            bits = bits | jnp.where(k < bcount[0, b], jnp.int32(1) << blist[0, b, k], 0)
        for s in range(9):
            tile = jnp.where(((bits >> s) & 1) == 1, e_v[b, s], jnp.zeros((TILE, TILE), BF16))
            u, v = s // 3, s % 3
            col = b + v
            if col in (1, 2):
                a_mid[u, b * TILE : (b + 1) * TILE, (col - 1) * TILE : col * TILE] = tile
            else:
                a_side[b, u] = tile

    def add_side(side, u):
        for b in range(2):
            acc[b * TILE : (b + 1) * TILE] += dot(a_side[b, u], side[b, u])

    acc[...] = dot(a_mid[1], pc[1])
    p_arrived("partner")
    acc[...] += dot(a_mid[u_in], pc[u_in])
    pl.semaphore_wait(entered.at[0], 4)
    tell(entered.at[2], "xy", 2)
    pl.semaphore_wait(entered.at[1], 2)
    tell(entered.at[3], "z", 2)
    for dv in (-1, 1):
        p_arrived(("outer", dv))
        p_start(("relay", dv))
    for dv in (-1, 1):
        p_arrived(("side", dv))
        p_start(("share", dv))
    add_side(ps, 1)
    acc[...] += dot(a_mid[u_out], pc[u_out])
    p_arrived(*shares)
    add_side(ps, u_in)
    p_arrived(*relays)
    add_side(ps, u_out)

    for half in range(2):
        ax[half] = acc[:, half * 256 : (half + 1) * 256].astype(BF16)
    ax_copy = pltpu.make_async_remote_copy(
        src_ref=ax.at[1 - core],
        dst_ref=axp,
        send_sem=ax_sem.at[0],
        recv_sem=ax_sem.at[1],
        device_id=partner,
        device_id_type=MESH,
    )
    ax_copy.start()
    loads[2].wait()
    acc[...] = dot(ax[0], w_v[:256]) + dot(ax[1], w_v[256:])
    loads[3].wait()
    for r in range(0, 256, 32):
        p = acc[r : r + 32]
        sig = jax.nn.sigmoid(p)
        hid_v[r : r + 32] = (p * sig).astype(BF16)
        g = gh_v[r : r + 32].astype(F32)
        qc[1, r : r + 32] = (g * sig * (1.0 + p * (1.0 - sig))).astype(BF16)

    q_start("partner")

    own_part = dot_rows(ax[core], qc[1])
    part[...] = own_part.reshape(2, 8, 16, 512)
    ax_copy.wait()

    q_arrived("partner")
    part[...] += dot_rows(axp[...], qc[u_in]).reshape(2, 8, 16, 512)
    s1[...] = part[...].astype(BF16)

    first = ("y", "x")
    second = ("x", "y")
    at = {"x": x, "y": y, "z": z}

    def ar(k, src, dst, dev):
        return pltpu.make_async_remote_copy(
            src_ref=src,
            dst_ref=dst,
            send_sem=ar_ss.at[k],
            recv_sem=ar_rs.at[k],
            device_id=dev,
            device_id_type=MESH,
        )

    sent = []
    far_first = (4, 3, 5, 2, 6, 1, 7)
    both = [(h, d) for d in far_first for h in range(2)]
    quarters = [(h, c) for h in range(2) for c in range(2)]

    def run(copies):
        for c in copies:
            c.start()
        sent.extend(copies)
        return copies

    def scatter(h, d):
        k, dev = peer(first[h], d)
        return ar(h * 7 + d - 1, s1.at[h, k], r1.at[h, d - 1], dev)

    def axis_of(stage, h, c):
        return "z" if stage == c else second[h]

    def exchange(stage, h, c, d):
        _, dev = peer(axis_of(stage, h, c), d)
        slot = rx.at[stage, h, c, at[axis_of(stage, h, c)]]
        return ar(14 + ((stage * 2 + h) * 2 + c) * 7 + d - 1, slot, slot, dev)

    def exchange_all(stage):
        return run([exchange(stage, h, c, d) for d in far_first for h, c in quarters])

    def summed(stage, h, c):
        total = rx[stage, h, c, 0].astype(F32)
        for k in range(1, 8):
            total = total + rx[stage, h, c, k].astype(F32)
        return total.astype(BF16)

    def gather(h, d):
        _, dev = peer(first[h], d)
        slot = t1.at[h, at[first[h]]]
        return ar(70 + h * 7 + d - 1, slot, slot, dev)

    pl.semaphore_wait(entered.at[2], 4)
    copies = run([scatter(h, d) for h, d in both])
    q_start(*outers, *sides)
    for c in copies:
        c.wait_recv()
    for h in range(2):
        total = part[h, at[first[h]]]
        for d in range(7):
            total = total + r1[h, d].astype(F32)
        for c in range(2):
            rx[1, h, c, at[axis_of(1, h, c)]] = total[:, c * 256 : (c + 1) * 256].astype(BF16)

    pl.semaphore_wait(entered.at[3], 2)
    copies = exchange_all(1)
    for dv in (-1, 1):
        q_arrived(("side", dv))
        q_start(("share", dv))
    for c in copies:
        c.wait_recv()
    for h, c in quarters:
        rx[0, h, c, at[axis_of(0, h, c)]] = summed(1, h, c)
    copies = exchange_all(0)
    for dv in (-1, 1):
        q_arrived(("outer", dv))
        q_start(("relay", dv))
    for c in copies:
        c.wait_recv()
    for h, c in quarters:
        t1[h, at[first[h]], :, c * 256 : (c + 1) * 256] = summed(0, h, c)
    copies = run([gather(h, d) for h, d in both])

    def pair(h, d):
        k = lax.rem(at[first[h]] + (8 - d), 8)
        c = pltpu.make_async_remote_copy(
            src_ref=t1.at[h, k],
            dst_ref=tp.at[h, k],
            send_sem=tp_ss.at[h * 8 + d],
            recv_sem=tp_rs.at[h * 8 + d],
            device_id=partner,
            device_id_type=MESH,
        )
        c.start()
        return c

    pairs = [pair(h, 0) for h in range(2)]
    acc[...] = dot(a_mid[0], qc[0]) + dot(a_mid[1], qc[1]) + dot(a_mid[2], qc[2])
    q_arrived(*shares)
    add_side(qs, 1)
    add_side(qs, u_in)

    for (h, d), c in sorted(zip(both, copies), key=lambda e: (min(e[0][1], 8 - e[0][1]), e[0])):
        c.wait_recv()
        pairs.append(pair(h, d))
    q_arrived(*relays)
    add_side(qs, u_out)
    back[...] = acc[...].astype(BF16)
    gf_v[...] = dot_cols(back[...], w_v[...]).astype(BF16)

    gw_v[core] = t1[...].astype(F32) * scale
    for c in pairs:
        c.wait_recv()
    gw_v[1 - core] = tp[...].astype(F32) * scale

    for c in sent + pairs:
        c.wait_send()
    p_drained()
    q_drained()


def write_out(hid_v, gf_v, gw_v, hid_o, gf_o, gw_o, sem):
    copies = [
        pltpu.make_async_copy(gw_v, gw_o, sem.at[0]),
        pltpu.make_async_copy(hid_v, hid_o, sem.at[1]),
        pltpu.make_async_copy(gf_v, gf_o, sem.at[2]),
    ]
    for copy in copies:
        copy.start()
    for copy in copies:
        copy.wait()


def per_device(features, weight, edge_tiles, block_list, block_count, grad_hidden):
    rows, width = 2 * TILE, features.shape[3]
    nodes = LOOP * SECTION * rows
    local = pl.BlockSpec(memory_space=pltpu.VMEM)
    anywhere = pl.BlockSpec(memory_space=pl.ANY)
    dma = pltpu.SemaphoreType.DMA
    vmem = pltpu.VMEM
    results = pl.pallas_call(
        functools.partial(kernel, 1.0 / math.sqrt(nodes)),
        out_shape=[
            pltpu.VMEM((rows, width), BF16),
            pltpu.VMEM((rows, width), BF16),
            pltpu.VMEM((2, 2, 8, 16, width), F32),
        ],
        in_specs=[anywhere] * 6,
        out_specs=[local] * 3,
        scratch_shapes=[
            vmem((width, width), BF16),
            vmem((2, 9, TILE, TILE), BF16),
            vmem((rows, width), BF16),
            vmem((3, rows, rows), BF16),
            vmem((2, 3, TILE, TILE), BF16),
            vmem((rows, width), F32),
            vmem((3, rows, width), BF16),
            vmem((2, 3, TILE, width), BF16),
            vmem((3, rows, width), BF16),
            vmem((2, 3, TILE, width), BF16),
            vmem((2, rows, 256), BF16),
            vmem((rows, 256), BF16),
            vmem((rows, width), BF16),
            vmem((2, 8, 16, width), F32),
            vmem((2, 8, 16, width), BF16),
            vmem((2, 7, 16, width), BF16),
            vmem((2, 2, 2, 8, 16, 256), BF16),
            vmem((2, 8, 16, width), BF16),
            vmem((2, 8, 16, width), BF16),
            pltpu.SMEM((1, 2, 9), jnp.int32),
            pltpu.SMEM((1, 2), jnp.int32),
            dma((6,)),
            dma((9,)),
            dma((9,)),
            dma((9,)),
            dma((9,)),
            dma((2,)),
            dma((84,)),
            dma((84,)),
            dma((16,)),
            dma((16,)),
            pltpu.SemaphoreType.REGULAR((4,)),
        ],
        compiler_params=pltpu.CompilerParams(collective_id=0, has_side_effects=True),
    )(
        block_list,
        block_count,
        features.reshape(rows, width),
        weight,
        edge_tiles.reshape(2, 9, TILE, TILE),
        grad_hidden.reshape(rows, width),
    )
    hidden, grad_features, grad_weight = pl.pallas_call(
        write_out,
        out_shape=[
            jax.ShapeDtypeStruct((rows, width), BF16),
            jax.ShapeDtypeStruct((rows, width), BF16),
            jax.ShapeDtypeStruct((2, 2, 8, 16, width), F32),
        ],
        in_specs=[local] * 3,
        out_specs=[anywhere] * 3,
        scratch_shapes=[dma((3,))],
    )(*[pltpu.with_memory_space_constraint(r, pltpu.VMEM) for r in results])
    grad_weight = grad_weight.reshape(width, width)
    return (hidden.reshape(features.shape), grad_features.reshape(features.shape), grad_weight)


def solution(mesh):
    placed = (
        P("loop", "section", None, None),
        P(),
        P("loop", "section", None, None, None),
        P("loop", "section", None),
        P("loop", "section"),
        P("loop", "section", None, None),
    )
    return jax.shard_map(
        per_device,
        mesh=mesh,
        in_specs=placed,
        out_specs=(P("loop", "section", None, None), P("loop", "section", None, None), P()),
        check_vma=False,
    )
```

```python
import functools
import math

import jax
import jax.numpy as jnp
from jax import lax
from jax.experimental import pallas as pl
from jax.experimental.pallas import tpu as pltpu
from jax.sharding import PartitionSpec as P

MESH = pl.DeviceIdType.MESH
F32 = jnp.float32
BF16 = jnp.bfloat16
TILE = 128
NX, NY, NZ, NYLO = 8, 8, 8, 4
LOOP, SECTION = 2 * NX * (NY // NYLO), NYLO * NZ


def dot(a, b):
    return jnp.dot(a, b, preferred_element_type=F32)


def dot_rows(a, b):
    return lax.dot_general(a, b, (((0,), (0,)), ((), ())), preferred_element_type=F32)


def dot_cols(a, b):
    return lax.dot_general(a, b, (((1,), (1,)), ((), ())), preferred_element_type=F32)


def kernel(
    scale,
    blist_h,
    bcount_h,
    feat,
    weight,
    edge,
    gh,
    hid_v,
    gf_v,
    gw_v,
    w_v,
    e_v,
    gh_v,
    a_mid,
    a_side,
    acc,
    pc,
    ps,
    qc,
    qs,
    ax,
    axp,
    back,
    part,
    s1,
    r1,
    rx,
    t1,
    tp,
    blist,
    bcount,
    in_sem,
    halo_ss,
    halo_rs,
    ghalo_ss,
    ghalo_rs,
    ax_sem,
    ar_ss,
    ar_rs,
    tp_ss,
    tp_rs,
    entered,
):
    L = lax.axis_index("loop")
    S = lax.axis_index("section")
    core = lax.rem(L, 2)
    x = lax.rem(L // 2, NX)
    y = (L // (2 * NX)) * NYLO + S // NZ
    z = lax.rem(S, NZ)

    def place(px, py, pz):
        return ((py // NYLO) * (2 * NX) + px * 2 + core, lax.rem(py, NYLO) * NZ + pz)

    def peer(axis, d):
        if axis == "x":
            k = lax.rem(x + d, NX)
            return k, place(k, y, z)
        if axis == "y":
            k = lax.rem(y + d, NY)
            return k, place(x, k, z)
        k = lax.rem(z + d, NZ)
        return k, place(x, y, k)

    out_row = L - 1 + 2 * core
    partner = (L + 1 - 2 * core, S)
    has_out = (out_row >= 0) & (out_row < LOOP)
    has_side = {-1: S > 0, 1: S < SECTION - 1}
    u_out, u_in = 2 * core, 2 * (1 - core)

    barrier = pltpu.get_barrier_semaphore()
    pl.semaphore_signal(barrier, inc=1, device_id=partner, device_id_type=MESH)

    @pl.when(has_out)
    def _():
        pl.semaphore_signal(barrier, inc=1, device_id=(out_row, S), device_id_type=MESH)

    for dv in (-1, 1):

        @pl.when(has_side[dv])
        def _(dv=dv):
            pl.semaphore_signal(barrier, inc=1, device_id=(L, S + dv), device_id_type=MESH)

    def tell(sem, axes, hops):
        for axis in axes:
            for d in (hops, 8 - hops):
                pl.semaphore_signal(sem, inc=1, device_id=peer(axis, d)[1], device_id_type=MESH)

    tell(barrier, "xyz", 1)

    loads = [
        pltpu.make_async_copy(feat, pc.at[1], in_sem.at[0]),
        pltpu.make_async_copy(edge, e_v, in_sem.at[1]),
        pltpu.make_async_copy(weight, w_v, in_sem.at[2]),
        pltpu.make_async_copy(gh, gh_v, in_sem.at[3]),
        pltpu.make_async_copy(blist_h, blist, in_sem.at[4]),
        pltpu.make_async_copy(bcount_h, bcount, in_sem.at[5]),
    ]
    for load in loads:
        load.start()

    for mid, side in ((pc, ps), (qc, qs)):

        @pl.when(jnp.logical_not(has_out))
        def _(mid=mid, side=side):
            mid[u_out] = jnp.zeros((2 * TILE, 512), BF16)
            for k in range(2):
                side[k, u_out] = jnp.zeros((TILE, 512), BF16)

        for dv, k in ((-1, 0), (1, 1)):

            @pl.when(jnp.logical_not(has_side[dv]))
            def _(side=side, k=k):
                side[k] = jnp.zeros((3, TILE, 512), BF16)

    def halo(mid, side, ss, rs):
        def copy(n, src, dst, dev):
            return pltpu.make_async_remote_copy(
                src_ref=src,
                dst_ref=dst,
                send_sem=ss.at[n],
                recv_sem=rs.at[n],
                device_id=dev,
                device_id_type=MESH,
            )

        cut = {-1: pl.ds(0, TILE), 1: pl.ds(TILE, TILE)}
        slot = {-1: 1, 1: 0}
        jobs = {
            "partner": (copy(0, mid.at[1], mid.at[u_out], partner), None, None),
        }
        for i, dv in enumerate((-1, 1)):
            dev = (L, S + dv)
            jobs["outer", dv] = (
                copy((1, 8)[i], mid.at[1, cut[dv]], mid.at[u_in, cut[dv]], (out_row, S)),
                has_out,
                has_out,
            )
            jobs["side", dv] = (
                copy(2 + i, mid.at[1, cut[dv]], side.at[slot[dv], 1], dev),
                has_side[dv],
                has_side[-dv],
            )
            jobs["relay", dv] = (
                copy(4 + i, mid.at[u_out, cut[dv]], side.at[slot[dv], u_out], dev),
                has_side[dv] & has_out,
                has_side[-dv] & has_out,
            )
            jobs["share", dv] = (
                copy(6 + i, side.at[slot[dv], 1], side.at[slot[dv], u_out], partner),
                has_side[-dv],
                has_side[-dv],
            )

        def start(*keys):
            for key in keys:
                job, sends, _ = jobs[key]
                job.start() if sends is None else pl.when(sends)(job.start)

        def arrived(*keys):
            for key in keys:
                job, _, gets = jobs[key]
                job.wait_recv() if gets is None else pl.when(gets)(job.wait_recv)

        def drained():
            for job, sends, _ in jobs.values():
                job.wait_send() if sends is None else pl.when(sends)(job.wait_send)

        return start, arrived, drained

    p_start, p_arrived, p_drained = halo(pc, ps, halo_ss, halo_rs)
    q_start, q_arrived, q_drained = halo(qc, qs, ghalo_ss, ghalo_rs)
    sides = (("side", -1), ("side", 1))
    relays = (("relay", -1), ("relay", 1))
    shares = (("share", -1), ("share", 1))
    outers = (("outer", -1), ("outer", 1))

    loads[0].wait()
    greeted = has_out.astype(jnp.int32) + sum(has_side[dv].astype(jnp.int32) for dv in (-1, 1))
    pl.semaphore_wait(barrier, 7 + greeted)
    p_start(*outers, *sides, "partner")
    tell(entered.at[0], "xy", 1)
    tell(entered.at[1], "z", 1)

    for k in (1, 4, 5):
        loads[k].wait()
    for b in range(2):
        bits = jnp.int32(0)
        for k in range(9):
            bits = bits | jnp.where(k < bcount[0, b], jnp.int32(1) << blist[0, b, k], 0)
        for s in range(9):
            tile = jnp.where(((bits >> s) & 1) == 1, e_v[b, s], jnp.zeros((TILE, TILE), BF16))
            u, v = s // 3, s % 3
            col = b + v
            if col in (1, 2):
                a_mid[u, b * TILE : (b + 1) * TILE, (col - 1) * TILE : col * TILE] = tile
            else:
                a_side[b, u] = tile

    def add_side(side, u):
        for b in range(2):
            acc[b * TILE : (b + 1) * TILE] += dot(a_side[b, u], side[b, u])

    acc[...] = dot(a_mid[1], pc[1])
    p_arrived("partner")
    acc[...] += dot(a_mid[u_in], pc[u_in])
    pl.semaphore_wait(entered.at[0], 4)
    tell(entered.at[2], "xy", 2)
    pl.semaphore_wait(entered.at[1], 2)
    tell(entered.at[3], "z", 2)
    for dv in (-1, 1):
        p_arrived(("outer", dv))
        p_start(("relay", dv))
    for dv in (-1, 1):
        p_arrived(("side", dv))
        p_start(("share", dv))
    add_side(ps, 1)
    acc[...] += dot(a_mid[u_out], pc[u_out])
    p_arrived(*shares)
    add_side(ps, u_in)
    p_arrived(*relays)
    add_side(ps, u_out)

    for half in range(2):
        ax[half] = acc[:, half * 256 : (half + 1) * 256].astype(BF16)
    ax_copy = pltpu.make_async_remote_copy(
        src_ref=ax.at[1 - core],
        dst_ref=axp,
        send_sem=ax_sem.at[0],
        recv_sem=ax_sem.at[1],
        device_id=partner,
        device_id_type=MESH,
    )
    ax_copy.start()
    loads[2].wait()
    acc[...] = dot(ax[0], w_v[:256]) + dot(ax[1], w_v[256:])
    loads[3].wait()
    for r in range(0, 256, 32):
        p = acc[r : r + 32]
        sig = jax.nn.sigmoid(p)
        hid_v[r : r + 32] = (p * sig).astype(BF16)
        g = gh_v[r : r + 32].astype(F32)
        qc[1, r : r + 32] = (g * sig * (1.0 + p * (1.0 - sig))).astype(BF16)

    q_start("partner")

    own_part = dot_rows(ax[core], qc[1])
    part[...] = own_part.reshape(2, 8, 16, 512)
    ax_copy.wait()

    q_arrived("partner")
    part[...] += dot_rows(axp[...], qc[u_in]).reshape(2, 8, 16, 512)
    s1[...] = part[...].astype(BF16)

    first = ("y", "x")
    second = ("x", "y")
    at = {"x": x, "y": y, "z": z}

    def ar(k, src, dst, dev):
        return pltpu.make_async_remote_copy(
            src_ref=src,
            dst_ref=dst,
            send_sem=ar_ss.at[k],
            recv_sem=ar_rs.at[k],
            device_id=dev,
            device_id_type=MESH,
        )

    sent = []
    far_first = (4, 3, 5, 2, 6, 1, 7)
    both = [(h, d) for d in far_first for h in range(2)]
    quarters = [(h, c) for h in range(2) for c in range(2)]

    def run(copies):
        for c in copies:
            c.start()
        sent.extend(copies)
        return copies

    def scatter(h, d):
        k, dev = peer(first[h], d)
        return ar(h * 7 + d - 1, s1.at[h, k], r1.at[h, d - 1], dev)

    def axis_of(stage, h, c):
        return "z" if stage == c else second[h]

    def exchange(stage, h, c, d):
        _, dev = peer(axis_of(stage, h, c), d)
        slot = rx.at[stage, h, c, at[axis_of(stage, h, c)]]
        return ar(14 + ((stage * 2 + h) * 2 + c) * 7 + d - 1, slot, slot, dev)

    def exchange_all(stage):
        return run([exchange(stage, h, c, d) for d in far_first for h, c in quarters])

    def summed(stage, h, c):
        total = rx[stage, h, c, 0].astype(F32)
        for k in range(1, 8):
            total = total + rx[stage, h, c, k].astype(F32)
        return total.astype(BF16)

    def gather(h, d):
        _, dev = peer(first[h], d)
        slot = t1.at[h, at[first[h]]]
        return ar(70 + h * 7 + d - 1, slot, slot, dev)

    pl.semaphore_wait(entered.at[2], 4)
    copies = run([scatter(h, d) for h, d in both])
    q_start(*outers, *sides)
    for c in copies:
        c.wait_recv()
    for h in range(2):
        total = part[h, at[first[h]]]
        for d in range(7):
            total = total + r1[h, d].astype(F32)
        for c in range(2):
            rx[1, h, c, at[axis_of(1, h, c)]] = total[:, c * 256 : (c + 1) * 256].astype(BF16)

    pl.semaphore_wait(entered.at[3], 2)
    copies = exchange_all(1)
    for dv in (-1, 1):
        q_arrived(("side", dv))
        q_start(("share", dv))
    for c in copies:
        c.wait_recv()
    for h, c in quarters:
        rx[0, h, c, at[axis_of(0, h, c)]] = summed(1, h, c)
    copies = exchange_all(0)

    def q_corners():
        for dv in (-1, 1):
            q_arrived(("outer", dv))
            q_start(("relay", dv))

    border = ((x == NX - 1) & (core == 1)) | ((x == 0) & (core == 0))
    pl.when(jnp.logical_not(border))(q_corners)
    for c in copies:
        c.wait_recv()
    for h, c in quarters:
        t1[h, at[first[h]], :, c * 256 : (c + 1) * 256] = summed(0, h, c)
    copies = run([gather(h, d) for h, d in both])

    def pair(h, d):
        k = lax.rem(at[first[h]] + (8 - d), 8)
        c = pltpu.make_async_remote_copy(
            src_ref=t1.at[h, k],
            dst_ref=tp.at[h, k],
            send_sem=tp_ss.at[h * 8 + d],
            recv_sem=tp_rs.at[h * 8 + d],
            device_id=partner,
            device_id_type=MESH,
        )
        c.start()
        return c

    pairs = [pair(h, 0) for h in range(2)]
    pl.when(border)(q_corners)
    acc[...] = dot(a_mid[0], qc[0]) + dot(a_mid[1], qc[1]) + dot(a_mid[2], qc[2])
    q_arrived(*shares)
    add_side(qs, 1)
    add_side(qs, u_in)

    for (h, d), c in sorted(zip(both, copies), key=lambda e: (min(e[0][1], 8 - e[0][1]), e[0])):
        c.wait_recv()
        pairs.append(pair(h, d))
    q_arrived(*relays)
    add_side(qs, u_out)
    back[...] = acc[...].astype(BF16)
    gf_v[...] = dot_cols(back[...], w_v[...]).astype(BF16)

    gw_v[core] = t1[...].astype(F32) * scale
    for c in pairs:
        c.wait_recv()
    gw_v[1 - core] = tp[...].astype(F32) * scale

    for c in sent + pairs:
        c.wait_send()
    p_drained()
    q_drained()


def write_out(hid_v, gf_v, gw_v, hid_o, gf_o, gw_o, sem):
    copies = [
        pltpu.make_async_copy(gw_v, gw_o, sem.at[0]),
        pltpu.make_async_copy(hid_v, hid_o, sem.at[1]),
        pltpu.make_async_copy(gf_v, gf_o, sem.at[2]),
    ]
    for copy in copies:
        copy.start()
    for copy in copies:
        copy.wait()


def per_device(features, weight, edge_tiles, block_list, block_count, grad_hidden):
    rows, width = 2 * TILE, features.shape[3]
    nodes = LOOP * SECTION * rows
    local = pl.BlockSpec(memory_space=pltpu.VMEM)
    anywhere = pl.BlockSpec(memory_space=pl.ANY)
    dma = pltpu.SemaphoreType.DMA
    vmem = pltpu.VMEM
    results = pl.pallas_call(
        functools.partial(kernel, 1.0 / math.sqrt(nodes)),
        out_shape=[
            pltpu.VMEM((rows, width), BF16),
            pltpu.VMEM((rows, width), BF16),
            pltpu.VMEM((2, 2, 8, 16, width), F32),
        ],
        in_specs=[anywhere] * 6,
        out_specs=[local] * 3,
        scratch_shapes=[
            vmem((width, width), BF16),
            vmem((2, 9, TILE, TILE), BF16),
            vmem((rows, width), BF16),
            vmem((3, rows, rows), BF16),
            vmem((2, 3, TILE, TILE), BF16),
            vmem((rows, width), F32),
            vmem((3, rows, width), BF16),
            vmem((2, 3, TILE, width), BF16),
            vmem((3, rows, width), BF16),
            vmem((2, 3, TILE, width), BF16),
            vmem((2, rows, 256), BF16),
            vmem((rows, 256), BF16),
            vmem((rows, width), BF16),
            vmem((2, 8, 16, width), F32),
            vmem((2, 8, 16, width), BF16),
            vmem((2, 7, 16, width), BF16),
            vmem((2, 2, 2, 8, 16, 256), BF16),
            vmem((2, 8, 16, width), BF16),
            vmem((2, 8, 16, width), BF16),
            pltpu.SMEM((1, 2, 9), jnp.int32),
            pltpu.SMEM((1, 2), jnp.int32),
            dma((6,)),
            dma((9,)),
            dma((9,)),
            dma((9,)),
            dma((9,)),
            dma((2,)),
            dma((84,)),
            dma((84,)),
            dma((16,)),
            dma((16,)),
            pltpu.SemaphoreType.REGULAR((4,)),
        ],
        compiler_params=pltpu.CompilerParams(collective_id=0, has_side_effects=True),
    )(
        block_list,
        block_count,
        features.reshape(rows, width),
        weight,
        edge_tiles.reshape(2, 9, TILE, TILE),
        grad_hidden.reshape(rows, width),
    )
    hidden, grad_features, grad_weight = pl.pallas_call(
        write_out,
        out_shape=[
            jax.ShapeDtypeStruct((rows, width), BF16),
            jax.ShapeDtypeStruct((rows, width), BF16),
            jax.ShapeDtypeStruct((2, 2, 8, 16, width), F32),
        ],
        in_specs=[local] * 3,
        out_specs=[anywhere] * 3,
        scratch_shapes=[dma((3,))],
    )(*[pltpu.with_memory_space_constraint(r, pltpu.VMEM) for r in results])
    grad_weight = grad_weight.reshape(width, width)
    return (hidden.reshape(features.shape), grad_features.reshape(features.shape), grad_weight)


def solution(mesh):
    placed = (
        P("loop", "section", None, None),
        P(),
        P("loop", "section", None, None, None),
        P("loop", "section", None),
        P("loop", "section"),
        P("loop", "section", None, None),
    )
    return jax.shard_map(
        per_device,
        mesh=mesh,
        in_specs=placed,
        out_specs=(P("loop", "section", None, None), P("loop", "section", None, None), P()),
        check_vma=False,
    )
```
